256 devices in a mesh: stn: 64 (over y_hi, z, x), beam: 4 (over y_lo, core).
Axes of the slice: x: 4, y: 4 (y_hi: 2, y_lo: 2; y = y_hi * 2 + y_lo), z: 8, core: 2. Of those that a mesh axis runs over, the one named last changes fastest.
Arguments:
- voltages: bfloat16 [512, 2, 614400], P(('stn', 'beam')), may hold values from -6 to 6
- fir_taps: float32 [12, 8192], replicated, may hold values from -1.75 to 1.75
- delays: float32 [64, 64, 512], P('stn', 'beam'), may hold values from -16 to 16
- taper: float32 [64, 512], replicated, may hold values from 0.5 to 2
- station_map: int32 [512], replicated, may hold values from 0 to 511, each once
- beam_order: int32 [64], replicated, may hold values from 0 to 63, each once
- owners: int32 [4], replicated, may hold values from 0 to 63
Outputs:
- beams_re: float32 [64, 4096, 128], P('beam', 'stn')
- beams_im: float32 [64, 4096, 128], P('beam', 'stn')
The draws below stay inside these ranges and needn't reach their ends.
Inputs may be any that keep to these rules, and one draw needn't show every extreme that they name: `station_map`: each station row holds a different physical station. `beam_order`: each beam slot forms a different beam.
All inputs are finite; a program needn't handle non-finite values.
Results may differ from the reference program's by a relative error of at most 0.0064.
Values may be sent and summed in bfloat16 or wider, within the bound.
No kernel may reach another device: no remote copies, remote signals or barrier semaphores. Data moves between devices by JAX's collectives and lax.ppermute only.
A program may use at most 128 MiB of HBM per device.

```python
import math
import jax
import jax.numpy as jnp
from jax import lax

P_SIZE = 64
Q = 128
TAPS = 12
POL = 2
BEAMS = 64
FRAMES = 64
NFFT = 8192
CHANNELS = 4096
CH_DEV = 64
STATIONS = 512
BEAMS_G = 16
GROUPS = 4
OWNERS = 64
N_STN = 64


def place_ends(drawn, own_key, smallest, largest):
    longest = drawn.shape.index(max(drawn.shape))
    spots = []
    for shift in (0, 1):
        where = [jax.random.randint(jax.random.fold_in(own_key, axis), (), 0, length) for axis, length in enumerate(drawn.shape)]
        where[longest] = (where[longest] + shift) % drawn.shape[longest]
        spots.append(tuple(where))
    return drawn.at[spots[0]].set(smallest).at[spots[1]].set(largest)


def levels(own_key, dims, pieces, smallest, high):
    level, own = 1.0, jax.random.fold_in(own_key, 6)
    for axis_at, blocks in pieces:
        steps = jnp.exp(jax.random.uniform(jax.random.fold_in(own, axis_at), (blocks,), jnp.float32, smallest / len(pieces), high / len(pieces)))
        level = level * jnp.repeat(steps, dims[axis_at] // blocks).reshape([-1 if axis == axis_at else 1 for axis in range(len(dims))])
    return level


def scatter_about(rng, dims, width, limit, pieces=(), kind=jnp.bfloat16):
    values = width * jax.random.normal(rng, dims, jnp.float32)
    if pieces:
        values = values * levels(rng, dims, pieces, -0.22, 0.18)
    return jnp.clip(values, -limit, limit).astype(kind)


def setup_inputs(seed: int = 0) -> dict:
    arg_keys = jax.random.split(jax.random.key(seed), 8)
    return {
        "voltages": scatter_about(arg_keys[0], (STATIONS, POL, (FRAMES + TAPS - 1) * NFFT), 1.0, 6.0, ((0, 256),)),
        "fir_taps": scatter_about(arg_keys[1], (TAPS, NFFT), TAPS ** -0.5, 1.75, (), jnp.float32),
        "delays": jnp.clip(jax.random.uniform(arg_keys[2], (OWNERS, BEAMS, STATIONS), jnp.float32, -16.0, 16.0) * levels(arg_keys[2], (OWNERS, BEAMS, STATIONS), ((0, 64), (1, 4)), -0.4, 0.0), -16.0, 16.0),
        "taper": jnp.clip(jnp.exp(jax.random.uniform(arg_keys[3], (BEAMS, STATIONS), jnp.float32, math.log(0.5), math.log(2.0))), 0.5, 2.0),
        "station_map": jax.random.permutation(arg_keys[4], STATIONS).astype(jnp.int32),
        "beam_order": jax.random.permutation(arg_keys[5], BEAMS).astype(jnp.int32),
        "owners": place_ends(jax.random.randint(arg_keys[6], (GROUPS,), 0, OWNERS), jax.random.fold_in(arg_keys[6], 1), 0, OWNERS - 1).astype(jnp.int32),
    }


TWO_PI = 2.0 * math.pi

def dft_tables():
    first_idx = jnp.arange(P_SIZE, dtype=jnp.int32)
    second_idx = jnp.arange(Q, dtype=jnp.int32)
    half_idx = jnp.arange(Q // 2, dtype=jnp.int32)
    first_angle = TWO_PI / P_SIZE * (first_idx[:, None] * first_idx[None, :] % P_SIZE).astype(jnp.float32)
    twist_angle = TWO_PI / (P_SIZE * Q) * (first_idx[:, None] * second_idx[None, :]).astype(jnp.float32)
    second_angle = TWO_PI / Q * (second_idx[:, None] * half_idx[None, :] % Q).astype(jnp.float32)
    return (jnp.cos(first_angle).astype(jnp.bfloat16), jnp.sin(first_angle).astype(jnp.bfloat16), jnp.cos(twist_angle), jnp.sin(twist_angle), jnp.cos(second_angle).astype(jnp.bfloat16), jnp.sin(second_angle).astype(jnp.bfloat16))

def beam_weights(delay_cols, gain_cols, chan_ids):
    phase = delay_cols[:, :, None] * chan_ids.astype(jnp.float32)[None, None, :] * (TWO_PI / (P_SIZE * Q))
    weight_re = (gain_cols[:, :, None] * jnp.cos(phase)).astype(jnp.bfloat16)
    weight_im = (-(gain_cols[:, :, None] * jnp.sin(phase))).astype(jnp.bfloat16)
    return (weight_re, weight_im)

def channelize(samples, fir_taps, tables):
    cos_one, sin_one, twist_cos, twist_sin, cos_two, sin_two = tables
    blocks = samples.reshape(POL, FRAMES + TAPS - 1, P_SIZE * Q).astype(jnp.float32)
    filtered = jnp.zeros((POL, FRAMES, P_SIZE * Q), jnp.float32)
    for tap_idx in range(TAPS):
        filtered = filtered + fir_taps[tap_idx] * blocks[:, tap_idx:tap_idx + FRAMES]
    folded = lax.optimization_barrier(filtered.astype(jnp.bfloat16))
    folded = folded.astype(jnp.float32).reshape(POL, FRAMES, P_SIZE, Q)
    first_re = jnp.einsum('pfnq,an->pfaq', folded, cos_one.astype(jnp.float32))
    first_im = -jnp.einsum('pfnq,an->pfaq', folded, sin_one.astype(jnp.float32))
    turned_re = (first_re * twist_cos + first_im * twist_sin).astype(jnp.bfloat16)
    turned_im = (first_im * twist_cos - first_re * twist_sin).astype(jnp.bfloat16)
    turned_re, turned_im = lax.optimization_barrier((turned_re, turned_im))
    turned_re = turned_re.astype(jnp.float32)
    turned_im = turned_im.astype(jnp.float32)
    cos_wide = cos_two.astype(jnp.float32)
    sin_wide = sin_two.astype(jnp.float32)
    chan_re = jnp.einsum('pfaq,qb->bapf', turned_re, cos_wide) + jnp.einsum('pfaq,qb->bapf', turned_im, sin_wide)
    chan_im = jnp.einsum('pfaq,qb->bapf', turned_im, cos_wide) - jnp.einsum('pfaq,qb->bapf', turned_re, sin_wide)
    return (chan_re.astype(jnp.bfloat16).reshape(CHANNELS, POL * FRAMES), chan_im.astype(jnp.bfloat16).reshape(CHANNELS, POL * FRAMES))

def reference(voltages, fir_taps, delays, taper, station_map, beam_order, owners):
    tables = dft_tables()
    chan_re, chan_im = lax.map(lambda samples: channelize(samples, fir_taps, tables), voltages)
    slot_ids = jnp.arange(BEAMS, dtype=jnp.int32)
    slot_owner = owners[slot_ids // BEAMS_G]
    slot_delay = delays[slot_owner, slot_ids]
    delay_rows = slot_delay[:, station_map]
    gain_rows = taper[beam_order][:, station_map]
    beam_scale = 1.0 / math.sqrt(P_SIZE * Q * STATIONS)

    def one_block(block_idx):
        first_chan = block_idx * CH_DEV
        part_re = lax.dynamic_slice_in_dim(chan_re, first_chan, CH_DEV, 1).astype(jnp.float32)
        part_im = lax.dynamic_slice_in_dim(chan_im, first_chan, CH_DEV, 1).astype(jnp.float32)
        chan_ids = first_chan + jnp.arange(CH_DEV, dtype=jnp.int32)
        weight_re, weight_im = beam_weights(delay_rows, gain_rows, chan_ids)
        weight_re = weight_re.astype(jnp.float32)
        weight_im = weight_im.astype(jnp.float32)
        beam_re = (jnp.einsum('jrk,rkc->jkc', weight_re, part_re) - jnp.einsum('jrk,rkc->jkc', weight_im, part_im)) * beam_scale
        beam_im = (jnp.einsum('jrk,rkc->jkc', weight_re, part_im) + jnp.einsum('jrk,rkc->jkc', weight_im, part_re)) * beam_scale
        return (beam_re, beam_im)
    block_re, block_im = lax.map(one_block, jnp.arange(N_STN, dtype=jnp.int32))
    beams_re = jnp.transpose(block_re, (1, 0, 2, 3)).reshape(BEAMS, CHANNELS, POL * FRAMES)
    beams_im = jnp.transpose(block_im, (1, 0, 2, 3)).reshape(BEAMS, CHANNELS, POL * FRAMES)
    return (beams_re, beams_im)
```

```python
import math

import jax
import jax.numpy as jnp
import ml_dtypes
import numpy as np
from jax import lax
from jax.experimental import pallas as pl
from jax.experimental.pallas import tpu as pltpu
from jax.sharding import Mesh
from jax.sharding import PartitionSpec as P

P_SIZE = 64
Q = 128
CHANNELS = 4096
TAPS = 12
FRAMES = 64
STATIONS = 512
TWO_PI = 2.0 * math.pi
F32 = jnp.float32
BF16 = jnp.bfloat16
VMEM_LIMIT = 56 << 20

AXES = ("yh", "zh", "zl", "x", "yl", "c")
SIZES = (2, 4, 2, 4, 2, 2)
TURN = ("yh", "zl", "x", "yl", "c")
MERGE = ("zh", "yl", "c")
FRAME_CHUNK = 16


def dft_tables():
    idx = np.arange(P_SIZE)
    wide = np.arange(Q)
    first = TWO_PI / P_SIZE * (idx[:, None] * idx[None, :] % P_SIZE)
    second = TWO_PI / Q * (wide[:, None] * idx[None, :] % Q)
    twist = TWO_PI / (P_SIZE * Q) * (idx[:, None] * wide[None, :])

    def narrow(x):
        return x.astype(np.float32).astype(ml_dtypes.bfloat16)

    cos_one, sin_one = narrow(np.cos(first)), narrow(np.sin(first))
    cos_two, sin_two = narrow(np.cos(second)).T, narrow(np.sin(second)).T
    one = np.zeros((2, 2, P_SIZE, P_SIZE, 2), ml_dtypes.bfloat16)
    for pol in range(2):
        one[pol, 0, :, :, pol] = cos_one
        one[pol, 1, :, :, pol] = -sin_one
    two = np.zeros((2, P_SIZE, 2, Q), ml_dtypes.bfloat16)
    two[0, :, 0], two[0, :, 1] = cos_two, sin_two
    two[1, :, 0], two[1, :, 1] = -sin_two, cos_two
    turn = np.stack((np.cos(twist), np.sin(twist))).astype(np.float32)
    return one.reshape(4 * P_SIZE, 2 * P_SIZE), turn, two.reshape(2 * P_SIZE, 2 * Q)


def channel_kernel(volts, taps, one, twist, two, out, folded, turned_re, turned_im, stage):
    def filter_rows(block, carry):
        row = pl.multiple_of(block * 16, 16)
        coeff = [taps[m, pl.ds(row, 16), :] for m in range(TAPS)]
        for chunk in range(FRAMES // FRAME_CHUNK):
            first = chunk * FRAME_CHUNK
            window = [
                volts[0, first + t, pl.ds(row, 16), :].astype(F32)
                for t in range(FRAME_CHUNK + TAPS - 1)
            ]
            for k in range(FRAME_CHUNK):
                acc = coeff[0] * window[k]
                for m in range(1, TAPS):
                    acc = acc + coeff[m] * window[k + m]
                frame = first + k
                lane = frame % 2 * Q
                folded[frame // 2, pl.ds(row, 16), lane : lane + Q] = acc.astype(BF16)
        return carry

    lax.fori_loop(0, 8, filter_rows, 0)

    def first_section(pair, carry):
        part = jnp.dot(one[...], folded[pair], preferred_element_type=F32)
        for pol in range(2):
            for half in range(2):
                lanes = slice(half * Q, (half + 1) * Q)
                re = part[pol * 128 : pol * 128 + 64, lanes]
                im = part[pol * 128 + 64 : pol * 128 + 128, lanes]
                row = pol * FRAMES + pair * 2 + half
                turned_re[pl.ds(row, 64, stride=128), :] = re * twist[0] + im * twist[1]
                turned_im[pl.ds(row, 64, stride=128), :] = im * twist[0] - re * twist[1]
        return carry

    lax.fori_loop(0, FRAMES // 2, first_section, 0)

    def second_section(j, carry):
        for i in range(16):
            row = pl.multiple_of((j * 16 + i) * 128, 128)
            right = jnp.concatenate(
                (
                    turned_re[pl.ds(row, 128), :].astype(BF16),
                    turned_im[pl.ds(row, 128), :].astype(BF16),
                ),
                axis=1,
            )
            part = lax.dot_general(
                two[...], right, (((1,), (1,)), ((), ())), preferred_element_type=F32
            )
            stage[0, pl.ds(i, 64, stride=16), :] = part[:64]
            stage[1, pl.ds(i, 64, stride=16), :] = part[64:]
        for b in range(64):
            yh, zh, zl, x = b // 32, b // 8 % 4, b // 4 % 2, b % 4
            for ri in range(2):
                out[yh, zl, x, j, zh, 0, ri] = stage[ri, b * 16 : (b + 1) * 16, :].astype(BF16)
        return carry

    lax.fori_loop(0, 4, second_section, 0)


def whole(*shape):
    return pl.BlockSpec(shape, lambda step: (0,) * len(shape))


def channelize(voltages, fir_taps):
    one, twist, two = dft_tables()
    volts = voltages.reshape(2, 2, 75 * P_SIZE, Q).transpose(0, 2, 1, 3).reshape(2, 75, 128, Q)
    taps = jnp.broadcast_to(fir_taps.reshape(TAPS, P_SIZE, 1, Q), (TAPS, P_SIZE, 2, Q))
    return pl.pallas_call(
        channel_kernel,
        grid=(2,),
        in_specs=[
            pl.BlockSpec((1, 75, 128, Q), lambda s: (s, 0, 0, 0)),
            whole(TAPS, 128, Q),
            whole(256, 128),
            whole(2, 64, Q),
            whole(128, 256),
        ],
        out_specs=pl.BlockSpec(
            (2, 2, 4, 4, 4, 1, 2, 16, 128), lambda s: (0, 0, 0, 0, 0, s, 0, 0, 0)
        ),
        out_shape=jax.ShapeDtypeStruct((2, 2, 4, 4, 4, 2, 2, 16, 128), BF16),
        scratch_shapes=[
            pltpu.VMEM((FRAMES // 2, 128, 256), BF16),
            pltpu.VMEM((64 * 128, Q), F32),
            pltpu.VMEM((64 * 128, Q), F32),
            pltpu.VMEM((2, 1024, 128), F32),
        ],
        compiler_params=pltpu.CompilerParams(vmem_limit_bytes=VMEM_LIMIT),
        name="channelize",
    )(volts, taps.reshape(TAPS, 128, Q), jnp.asarray(one), jnp.asarray(twist), jnp.asarray(two))


def beam_kernel(spectra, base, step, out, wide):
    for src in range(64):
        wide[src * 64 : (src + 1) * 64, :] = spectra[src, 0].astype(F32)
    cos_w, sin_w = base[0, 0], base[0, 1]
    cos_step, sin_step = step[0], step[1]
    for i in range(16):
        right = jnp.concatenate(
            [
                wide[pl.ds((s * 2 + ri) * 16 + i, 64, stride=64), :].astype(BF16)
                for ri in range(2)
                for s in range(2)
            ],
            axis=0,
        )
        cos_n, sin_n = cos_w.astype(BF16), sin_w.astype(BF16)
        left = jnp.concatenate(
            (
                jnp.concatenate((cos_n, sin_n), axis=1),
                jnp.concatenate((-sin_n, cos_n), axis=1),
            ),
            axis=0,
        )
        part = jnp.dot(left, right, preferred_element_type=F32)
        for ri in range(2):
            for group in range(4):
                row = ri * 64 + group * 16
                out[0, group, ri, i] = part[row : row + 16].astype(BF16)
        if i < 15:
            cos_w, sin_w = (
                cos_w * cos_step - sin_w * sin_step,
                sin_w * cos_step + cos_w * sin_step,
            )


def form_beams(spectra, base, step):
    return pl.pallas_call(
        beam_kernel,
        grid=(4,),
        in_specs=[
            pl.BlockSpec((64, 1, 64, 128), lambda zh: (0, zh, 0, 0)),
            pl.BlockSpec((1, 2, 64, 128), lambda zh: (zh, 0, 0, 0)),
            whole(2, 64, 128),
        ],
        out_specs=pl.BlockSpec((1, 4, 2, 16, 16, 128), lambda zh: (zh, 0, 0, 0, 0, 0)),
        out_shape=jax.ShapeDtypeStruct((4, 4, 2, 16, 16, 128), BF16),
        scratch_shapes=[pltpu.VMEM((64 * 64, 128), F32)],
        compiler_params=pltpu.CompilerParams(vmem_limit_bytes=VMEM_LIMIT),
        name="form_beams",
    )(spectra, base, step)


def merge_kernel(parts, out_re, out_im):
    scale = 1.0 / math.sqrt(P_SIZE * Q * STATIONS)
    for ri, out in ((0, out_re), (1, out_im)):
        for i in range(16):
            total = parts[0, 0, ri, i].astype(F32)
            for zh in range(1, 4):
                total = total + parts[zh, 0, ri, i].astype(F32)
            out[:, i, :] = total * scale


def merge(parts):
    spec = pl.BlockSpec((16, 16, 128), lambda j: (0, j, 0))
    shape = jax.ShapeDtypeStruct((16, 64, 128), F32)
    return pl.pallas_call(
        merge_kernel,
        grid=(4,),
        in_specs=[pl.BlockSpec((4, 1, 2, 16, 16, 128), lambda j: (0, j, 0, 0, 0, 0))],
        out_specs=[spec, spec],
        out_shape=[shape, shape],
        compiler_params=pltpu.CompilerParams(vmem_limit_bytes=VMEM_LIMIT),
        name="merge",
    )(parts)


def beam_model(delays, taper, station_map, beam_order, owners):
    yh, zh, zl, x, yl, c = [lax.axis_index(name) for name in AXES]
    stn_pos = ((yh * 4 + zh) * 2 + zl) * 4 + x
    beam_pos = yl * 2 + c
    kept = jnp.where(owners[beam_pos] == stn_pos, delays[0], 0.0)
    gains = taper[beam_order]
    phys = station_map.reshape(2, 4, 32, 2).transpose(1, 3, 0, 2).reshape(STATIONS)
    pick = (jnp.arange(STATIONS, dtype=jnp.int32)[:, None] == phys[None, :]).astype(F32)
    cols = jnp.dot(
        jnp.concatenate((kept, gains), axis=0), pick, precision=lax.Precision.HIGHEST
    )
    slots = kept.shape[0]
    by_zh = cols[:slots].reshape(slots, 4, 128).transpose(1, 0, 2)
    mine = lax.psum_scatter(by_zh, "zh", scatter_dimension=0, tiled=False)
    gain = lax.dynamic_slice_in_dim(cols[slots:], zh * 128, 128, 1)
    spread = lax.all_to_all(
        jnp.broadcast_to(mine[None], (16, slots, 128)), ("yh", "zl", "x"), 0, 0, tiled=True
    )
    owner = owners[beam_pos]
    source = (owner // 32 * 2 + owner // 4 % 2) * 4 + owner % 4
    chosen = lax.dynamic_index_in_dim(spread, source, 0, keepdims=False)
    delay = lax.all_gather(chosen, ("yl", "c"), axis=0, tiled=True)
    return delay, gain


def on_device(voltages, fir_taps, delays, taper, station_map, beam_order, owners):
    yh, zh, zl, x, yl, c = [lax.axis_index(name) for name in AXES]
    spectra = channelize(voltages, fir_taps)
    delay, gain = beam_model(delays, taper, station_map, beam_order, owners)
    first_chan = yh * 2048 + zl * 256 + x * 64 + (yl * 2 + c) * 16
    chans = (first_chan + 512 * jnp.arange(4, dtype=jnp.int32)).astype(F32)
    unit = TWO_PI / (P_SIZE * Q)
    phase = delay[None] * chans[:, None, None] * unit
    base = jnp.stack((gain * jnp.cos(phase), gain * jnp.sin(phase)), axis=1)
    step = jnp.stack((jnp.cos(delay * unit), jnp.sin(delay * unit)))
    turned = lax.all_to_all(spectra.reshape(64, 4, 64, 128), TURN, 0, 0, tiled=True)
    partial = form_beams(turned, base, step)
    parts = lax.all_to_all(partial.reshape(16, 2, 16, 16, 128), MERGE, 0, 0, tiled=True)
    out_re, out_im = merge(parts.reshape(4, 4, 2, 16, 16, 128))
    return (out_re, out_im)


def solution(mesh):
    torus = Mesh(mesh.devices.reshape(SIZES), AXES)
    stn, beam = AXES[:4], AXES[4:]
    return jax.shard_map(
        on_device,
        mesh=torus,
        in_specs=(P(AXES, None, None), P(), P(stn, beam, None), P(), P(), P(), P()),
        out_specs=(P(beam, stn, None), P(beam, stn, None)),
        check_vma=False,
    )
```

```python
import math

import jax
import jax.numpy as jnp
import ml_dtypes
import numpy as np
from jax import lax
from jax.experimental import pallas as pl
from jax.experimental.pallas import tpu as pltpu
from jax.sharding import Mesh
from jax.sharding import PartitionSpec as P

P_SIZE = 64
Q = 128
CHANNELS = 4096
TAPS = 12
FRAMES = 64
STATIONS = 512
TWO_PI = 2.0 * math.pi
F32 = jnp.float32
BF16 = jnp.bfloat16
VMEM_LIMIT = 56 << 20

AXES = ("yh", "zh", "zl", "x", "yl", "c")
SIZES = (2, 4, 2, 4, 2, 2)
TURN = ("yh", "zl", "x", "yl", "c")
MERGE = ("zh", "yl", "c")
FRAME_CHUNK = 16
TURN_ROWS = 136
STAGE_ROWS = 24
WIDE_ROWS = 40


def dft_tables():
    idx = np.arange(P_SIZE)
    wide = np.arange(Q)
    first = TWO_PI / P_SIZE * (idx[:, None] * idx[None, :] % P_SIZE)
    second = TWO_PI / Q * (wide[:, None] * idx[None, :] % Q)
    twist = TWO_PI / (P_SIZE * Q) * (idx[:, None] * wide[None, :])

    def narrow(x):
        return x.astype(np.float32).astype(ml_dtypes.bfloat16)

    cos_one, sin_one = narrow(np.cos(first)), narrow(np.sin(first))
    cos_two, sin_two = narrow(np.cos(second)).T, narrow(np.sin(second)).T
    one = np.zeros((2, 2, P_SIZE, P_SIZE, 2), ml_dtypes.bfloat16)
    for pol in range(2):
        one[pol, 0, :, :, pol] = cos_one
        one[pol, 1, :, :, pol] = -sin_one
    two = np.zeros((2, P_SIZE, 2, Q), ml_dtypes.bfloat16)
    two[0, :, 0], two[0, :, 1] = cos_two, sin_two
    two[1, :, 0], two[1, :, 1] = -sin_two, cos_two
    turn = np.stack((np.cos(twist), np.sin(twist))).astype(np.float32)
    return one.reshape(4 * P_SIZE, 2 * P_SIZE), turn, two.reshape(2 * P_SIZE, 2 * Q)


def channel_kernel(volts, taps, one, twist, two, *refs):
    out_lo, out_hi, coeff_rows, folded, turned_re, turned_im, stage = refs[-7:]
    block = pl.program_id(0)
    for pol in range(2):
        for m in range(TAPS):
            coeff_rows[m, pl.ds(pol, 8, stride=2), :] = taps[m]
    coeff = [coeff_rows[m] for m in range(TAPS)]
    row0 = pl.multiple_of(block * 16, 16)
    for chunk in range(FRAMES // FRAME_CHUNK):
        first = chunk * FRAME_CHUNK
        window = [volts[0, first + t].astype(F32) for t in range(FRAME_CHUNK + TAPS - 1)]
        for k in range(FRAME_CHUNK):
            acc = coeff[0] * window[k]
            for m in range(1, TAPS):
                acc = acc + coeff[m] * window[k + m]
            frame = first + k
            lane = frame % 2 * Q
            folded[frame // 2, pl.ds(row0, 16), lane : lane + Q] = acc.astype(BF16)

    def first_section(pair, carry):
        part = jnp.dot(one[...], folded[pair], preferred_element_type=F32)
        for pol in range(2):
            for half in range(2):
                lanes = slice(half * Q, (half + 1) * Q)
                re = part[pol * 128 : pol * 128 + 64, lanes]
                im = part[pol * 128 + 64 : pol * 128 + 128, lanes]
                row = pol * FRAMES + pair * 2 + half
                turned_re[pl.ds(row, 64, stride=TURN_ROWS), :] = re * twist[0] + im * twist[1]
                turned_im[pl.ds(row, 64, stride=TURN_ROWS), :] = im * twist[0] - re * twist[1]
        return carry

    def second_section(j, carry):
        for i in range(16):
            row = pl.multiple_of((j * 16 + i) * TURN_ROWS, 8)
            right = jnp.concatenate(
                (
                    turned_re[pl.ds(row, 128), :].astype(BF16),
                    turned_im[pl.ds(row, 128), :].astype(BF16),
                ),
                axis=1,
            )
            part = lax.dot_general(
                two[...], right, (((1,), (1,)), ((), ())), preferred_element_type=F32
            )
            for ri in range(2):
                rows = pl.ds(ri * 8 + i % 8, 64, stride=STAGE_ROWS)
                stage[i // 8, rows, :] = part[ri * 64 : ri * 64 + 64]
        for b in range(64):
            yh, zh, zl, x = b // 32, b // 8 % 4, b // 4 % 2, b % 4
            rows = slice(b * STAGE_ROWS, b * STAGE_ROWS + 16)
            out_lo[yh, zl, x, j, zh, 0] = stage[0, rows, :].astype(BF16)
            out_hi[yh, zl, x, j, zh, 0] = stage[1, rows, :].astype(BF16)
        return carry

    @pl.when(block == 7)
    def _():
        lax.fori_loop(0, FRAMES // 2, first_section, 0)
        lax.fori_loop(0, 4, second_section, 0)


def whole(*shape):
    return pl.BlockSpec(shape, lambda step: (0,) * len(shape))


def channelize(volts, taps, station, earlier=()):
    one, twist, two = dft_tables()
    out_spec = pl.BlockSpec(
        (2, 2, 4, 4, 4, 1, 16, 128), lambda r: (0, 0, 0, 0, 0, station, 0, 0)
    )
    out_shape = jax.ShapeDtypeStruct((2, 2, 4, 4, 4, 2, 16, 128), BF16)
    return pl.pallas_call(
        channel_kernel,
        grid=(8,),
        in_specs=[
            pl.BlockSpec((1, 75, 16, Q), lambda r: (station, 0, r, 0)),
            pl.BlockSpec((TAPS, 8, Q), lambda r: (0, r, 0)),
            whole(256, 128),
            whole(2, 64, Q),
            whole(128, 256),
        ]
        + [pl.BlockSpec(memory_space=pl.ANY)] * len(earlier),
        out_specs=[out_spec, out_spec],
        out_shape=[out_shape, out_shape],
        input_output_aliases={5: 0, 6: 1} if earlier else {},
        scratch_shapes=[
            pltpu.VMEM((TAPS, 16, Q), F32),
            pltpu.VMEM((FRAMES // 2, 128, 256), BF16),
            pltpu.VMEM((64 * TURN_ROWS, Q), F32),
            pltpu.VMEM((64 * TURN_ROWS, Q), F32),
            pltpu.VMEM((2, 64 * STAGE_ROWS, 128), F32),
        ],
        compiler_params=pltpu.CompilerParams(vmem_limit_bytes=VMEM_LIMIT),
        name="channelize",
    )(volts, taps, jnp.asarray(one), jnp.asarray(twist), jnp.asarray(two), *earlier)


def beam_kernel(spectra, base, step, out, wide):
    for src in range(64):
        wide[src * WIDE_ROWS : src * WIDE_ROWS + 32, :] = spectra[src, 0].astype(F32)
    cos_w, sin_w = base[0, 0], base[0, 1]
    cos_step, sin_step = step[0], step[1]
    for i in range(8):
        right = jnp.concatenate(
            [
                wide[pl.ds(s * 16 + ri * 8 + i, 64, stride=WIDE_ROWS), :].astype(BF16)
                for ri in range(2)
                for s in range(2)
            ],
            axis=0,
        )
        cos_n, sin_n = cos_w.astype(BF16), sin_w.astype(BF16)
        left = jnp.concatenate(
            (
                jnp.concatenate((cos_n, sin_n), axis=1),
                jnp.concatenate((-sin_n, cos_n), axis=1),
            ),
            axis=0,
        )
        part = jnp.dot(left, right, preferred_element_type=F32)
        for ri in range(2):
            for group in range(4):
                row = ri * 64 + group * 16
                out[0, group, ri, i] = part[row : row + 16].astype(BF16)
        if i < 7:
            cos_w, sin_w = (
                cos_w * cos_step - sin_w * sin_step,
                sin_w * cos_step + cos_w * sin_step,
            )


def form_beams(spectra, base, step):
    return pl.pallas_call(
        beam_kernel,
        grid=(4,),
        in_specs=[
            pl.BlockSpec((64, 1, 32, 128), lambda zh: (0, zh, 0, 0)),
            pl.BlockSpec((1, 2, 64, 128), lambda zh: (zh, 0, 0, 0)),
            whole(2, 64, 128),
        ],
        out_specs=pl.BlockSpec((1, 4, 2, 8, 16, 128), lambda zh: (zh, 0, 0, 0, 0, 0)),
        out_shape=jax.ShapeDtypeStruct((4, 4, 2, 8, 16, 128), BF16),
        scratch_shapes=[pltpu.VMEM((64 * WIDE_ROWS, 128), F32)],
        compiler_params=pltpu.CompilerParams(vmem_limit_bytes=VMEM_LIMIT),
        name="form_beams",
    )(spectra, base, step)


def merge_kernel(parts, *refs):
    scale = 1.0 / math.sqrt(P_SIZE * Q * STATIONS)
    for ri, out in enumerate(refs[-2:]):
        for i in range(8):
            total = parts[0, 0, ri, i].astype(F32)
            for zh in range(1, 4):
                total = total + parts[zh, 0, ri, i].astype(F32)
            out[:, i, :] = total * scale


def merge(parts, half, earlier=()):
    spec = pl.BlockSpec((16, 8, 128), lambda j: (0, 2 * j + half, 0))
    shape = jax.ShapeDtypeStruct((16, 64, 128), F32)
    return pl.pallas_call(
        merge_kernel,
        grid=(4,),
        in_specs=[pl.BlockSpec((4, 1, 2, 8, 16, 128), lambda j: (0, j, 0, 0, 0, 0))]
        + [pl.BlockSpec(memory_space=pl.ANY)] * len(earlier),
        out_specs=[spec, spec],
        out_shape=[shape, shape],
        input_output_aliases={1: 0, 2: 1} if earlier else {},
        compiler_params=pltpu.CompilerParams(vmem_limit_bytes=VMEM_LIMIT),
        name="merge",
    )(parts, *earlier)


def station_pick(station_map):
    phys = station_map.reshape(2, 4, 32, 2).transpose(1, 3, 0, 2).reshape(STATIONS)
    return (jnp.arange(STATIONS, dtype=jnp.int32)[:, None] == phys[None, :]).astype(F32)


def pick_columns(values, pick):
    return jnp.dot(values, pick, precision=lax.Precision.HIGHEST)


def on_device(voltages, fir_taps, delays, taper, station_map, beam_order, owners):
    yh, zh, zl, x, yl, c = [lax.axis_index(name) for name in AXES]
    volts = voltages.reshape(2, 2, 75 * P_SIZE, Q).transpose(0, 2, 1, 3).reshape(2, 75, 128, Q)
    taps = fir_taps.reshape(TAPS, P_SIZE, Q)
    slots = delays.shape[1]

    pick = station_pick(station_map)
    model = pick_columns(delays[0], pick).reshape(slots, 4, 128).transpose(1, 0, 2)
    model = jnp.broadcast_to(model[None, :, None], (2, 4, 8, slots, 128))
    models = lax.all_to_all(model.reshape(64, slots, 128), AXES[:4], 0, 0, tiled=True)
    spectra = channelize(volts, taps, 0)
    models, spectra = lax.optimization_barrier((models, spectra))
    delay = lax.dynamic_index_in_dim(models, owners[yl * 2 + c], 0, keepdims=False)
    delay = lax.all_to_all(
        jnp.broadcast_to(delay[None], (4, slots, 128)), ("yl", "c"), 0, 0, tiled=True
    ).reshape(4 * slots, 128)
    spectra = channelize(volts, taps, 1, spectra)
    delay, lo, hi = lax.optimization_barrier((delay, *spectra))

    turned = [
        lax.all_to_all(half.reshape(64, 4, 32, 128), TURN, 0, 0, tiled=True) for half in (lo, hi)
    ]
    gain = pick_columns(taper[beam_order], pick)
    gain = lax.dynamic_slice_in_dim(gain, zh * 128, 128, 1)
    first_chan = yh * 2048 + zl * 256 + x * 64 + (yl * 2 + c) * 16
    unit = TWO_PI / (P_SIZE * Q)
    step = jnp.stack((jnp.cos(delay * unit), jnp.sin(delay * unit)))
    sums = []
    for half in range(2):
        chans = (first_chan + 8 * half + 512 * jnp.arange(4, dtype=jnp.int32)).astype(F32)
        phase = delay[None] * chans[:, None, None] * unit
        base = jnp.stack((gain * jnp.cos(phase), gain * jnp.sin(phase)), axis=1)
        partial = form_beams(turned[half], base, step)
        parts = lax.all_to_all(partial.reshape(16, 2, 8, 16, 128), MERGE, 0, 0, tiled=True)
        sums.append(parts.reshape(4, 4, 2, 8, 16, 128))
    out_re, out_im = merge(sums[1], 1, merge(sums[0], 0))
    return (out_re, out_im)


def solution(mesh):
    torus = Mesh(mesh.devices.reshape(SIZES), AXES)
    stn, beam = AXES[:4], AXES[4:]
    return jax.shard_map(
        on_device,
        mesh=torus,
        in_specs=(P(AXES, None, None), P(), P(stn, beam, None), P(), P(), P(), P()),
        out_specs=(P(beam, stn, None), P(beam, stn, None)),
        check_vma=False,
    )
```

```python
import math

import jax
import jax.numpy as jnp
import ml_dtypes
import numpy as np
from jax import lax
from jax.experimental import pallas as pl
from jax.experimental.pallas import tpu as pltpu
from jax.sharding import Mesh
from jax.sharding import PartitionSpec as P

P_SIZE = 64
Q = 128
CHANNELS = 4096
TAPS = 12
FRAMES = 64
STATIONS = 512
TWO_PI = 2.0 * math.pi
F32 = jnp.float32
BF16 = jnp.bfloat16
VMEM_LIMIT = 56 << 20

AXES = ("yh", "zh", "zl", "x", "yl", "c")
SIZES = (2, 4, 2, 4, 2, 2)
TURN = ("yh", "zl", "x", "yl", "c")
FRAME_CHUNK = 16
TURN_ROWS = 136
STAGE_ROWS = 40
WIDE_ROWS = 72
BEAM_ROWS = 24


def dft_tables():
    idx = np.arange(P_SIZE)
    wide = np.arange(Q)
    first = TWO_PI / P_SIZE * (idx[:, None] * idx[None, :] % P_SIZE)
    second = TWO_PI / Q * (wide[:, None] * idx[None, :] % Q)
    twist = TWO_PI / (P_SIZE * Q) * (idx[:, None] * wide[None, :])

    def narrow(x):
        return x.astype(np.float32).astype(ml_dtypes.bfloat16)

    cos_one, sin_one = narrow(np.cos(first)), narrow(np.sin(first))
    cos_two, sin_two = narrow(np.cos(second)).T, narrow(np.sin(second)).T
    one = np.zeros((2, 2, P_SIZE, P_SIZE, 2), ml_dtypes.bfloat16)
    for pol in range(2):
        one[pol, 0, :, :, pol] = cos_one
        one[pol, 1, :, :, pol] = -sin_one
    two = np.zeros((2, P_SIZE, 2, Q), ml_dtypes.bfloat16)
    two[0, :, 0], two[0, :, 1] = cos_two, sin_two
    two[1, :, 0], two[1, :, 1] = -sin_two, cos_two
    turn = np.stack((np.cos(twist), np.sin(twist))).astype(np.float32)
    return one.reshape(4 * P_SIZE, 2 * P_SIZE), turn, two.reshape(2 * P_SIZE, 2 * Q)


def channel_kernel(
    volts, taps, one, twist, two, out, coeff_rows, folded, turned_re, turned_im, stage
):
    block = pl.program_id(1)
    for pol in range(2):
        for m in range(TAPS):
            coeff_rows[m, pl.ds(pol, 8, stride=2), :] = taps[m]
    coeff = [coeff_rows[m] for m in range(TAPS)]
    row0 = pl.multiple_of(block * 16, 16)
    for chunk in range(FRAMES // FRAME_CHUNK):
        first = chunk * FRAME_CHUNK
        window = [volts[0, first + t].astype(F32) for t in range(FRAME_CHUNK + TAPS - 1)]
        for k in range(FRAME_CHUNK):
            acc = coeff[0] * window[k]
            for m in range(1, TAPS):
                acc = acc + coeff[m] * window[k + m]
            frame = first + k
            lane = frame % 2 * Q
            folded[frame // 2, pl.ds(row0, 16), lane : lane + Q] = acc.astype(BF16)

    def first_section(pair, carry):
        part = jnp.dot(one[...], folded[pair], preferred_element_type=F32)
        for pol in range(2):
            for half in range(2):
                lanes = slice(half * Q, (half + 1) * Q)
                re = part[pol * 128 : pol * 128 + 64, lanes]
                im = part[pol * 128 + 64 : pol * 128 + 128, lanes]
                row = pol * FRAMES + pair * 2 + half
                turned_re[pl.ds(row, 64, stride=TURN_ROWS), :] = re * twist[0] + im * twist[1]
                turned_im[pl.ds(row, 64, stride=TURN_ROWS), :] = im * twist[0] - re * twist[1]
        return carry

    def second_section(j, carry):
        for i in range(16):
            row = pl.multiple_of((j * 16 + i) * TURN_ROWS, 8)
            right = jnp.concatenate(
                (
                    turned_re[pl.ds(row, 128), :].astype(BF16),
                    turned_im[pl.ds(row, 128), :].astype(BF16),
                ),
                axis=1,
            )
            part = lax.dot_general(
                two[...], right, (((1,), (1,)), ((), ())), preferred_element_type=F32
            )
            for ri in range(2):
                rows = pl.ds(ri * 16 + i, 64, stride=STAGE_ROWS)
                stage[rows, :] = part[ri * 64 : ri * 64 + 64]
        for b in range(64):
            yh, zh, zl, x = b // 32, b // 8 % 4, b // 4 % 2, b % 4
            rows = slice(b * STAGE_ROWS, b * STAGE_ROWS + 32)
            out[yh, zl, x, j, zh, 0] = stage[rows, :].astype(BF16)
        return carry

    @pl.when(block == 7)
    def _():
        lax.fori_loop(0, FRAMES // 2, first_section, 0)
        lax.fori_loop(0, 4, second_section, 0)


def whole(*shape):
    return pl.BlockSpec(shape, lambda *step: (0,) * len(shape))


def channelize(volts, taps):
    one, twist, two = dft_tables()
    return pl.pallas_call(
        channel_kernel,
        grid=(2, 8),
        in_specs=[
            pl.BlockSpec((1, 75, 16, Q), lambda s, r: (s, 0, r, 0)),
            pl.BlockSpec((TAPS, 8, Q), lambda s, r: (0, r, 0)),
            whole(256, 128),
            whole(2, 64, Q),
            whole(128, 256),
        ],
        out_specs=pl.BlockSpec((2, 2, 4, 4, 4, 1, 32, 128), lambda s, r: (0, 0, 0, 0, 0, s, 0, 0)),
        out_shape=jax.ShapeDtypeStruct((2, 2, 4, 4, 4, 2, 32, 128), BF16),
        scratch_shapes=[
            pltpu.VMEM((TAPS, 16, Q), F32),
            pltpu.VMEM((FRAMES // 2, 128, 256), BF16),
            pltpu.VMEM((64 * TURN_ROWS, Q), F32),
            pltpu.VMEM((64 * TURN_ROWS, Q), F32),
            pltpu.VMEM((64 * STAGE_ROWS, 128), F32),
        ],
        compiler_params=pltpu.CompilerParams(vmem_limit_bytes=VMEM_LIMIT),
        name="channelize",
    )(volts, taps, jnp.asarray(one), jnp.asarray(twist), jnp.asarray(two))


def beam_kernel(where, spectra, base, step, out, wide):
    del where
    for src in range(64):
        wide[src * WIDE_ROWS : src * WIDE_ROWS + 64, :] = spectra[src, 0].astype(F32)
    cos_w, sin_w = base[0], base[1]
    cos_step, sin_step = step[0], step[1]
    for i in range(16):
        right = jnp.concatenate(
            [
                wide[pl.ds(s * 32 + ri * 16 + i, 64, stride=WIDE_ROWS), :].astype(BF16)
                for ri in range(2)
                for s in range(2)
            ],
            axis=0,
        )
        cos_n, sin_n = cos_w.astype(BF16), sin_w.astype(BF16)
        left = jnp.concatenate(
            (
                jnp.concatenate((cos_n, sin_n), axis=1),
                jnp.concatenate((-sin_n, cos_n), axis=1),
            ),
            axis=0,
        )
        part = jnp.dot(left, right, preferred_element_type=F32)
        for ri in range(2):
            for group in range(4):
                row = ri * 64 + group * 16
                out[group, ri, i] = part[row : row + 16].astype(BF16)
        if i < 15:
            cos_w, sin_w = (
                cos_w * cos_step - sin_w * sin_step,
                sin_w * cos_step + cos_w * sin_step,
            )


def form_beams(where, spectra, base, step):
    return pl.pallas_call(
        beam_kernel,
        grid_spec=pltpu.PrefetchScalarGridSpec(
            num_scalar_prefetch=1,
            grid=(1,),
            in_specs=[
                pl.BlockSpec((64, 1, 64, 128), lambda n, zh: (0, zh[0], 0, 0)),
                whole(2, 64, 128),
                whole(2, 64, 128),
            ],
            out_specs=whole(4, 2, 16, 16, 128),
            scratch_shapes=[pltpu.VMEM((64 * WIDE_ROWS, 128), F32)],
        ),
        out_shape=jax.ShapeDtypeStruct((4, 2, 16, 16, 128), BF16),
        compiler_params=pltpu.CompilerParams(vmem_limit_bytes=VMEM_LIMIT),
        name="form_beams",
    )(where, spectra, base, step)


def add_kernel(group, *refs):
    del group
    total = refs[0][0].astype(F32)
    for part in refs[1:-1]:
        total = total + part[0].astype(F32)
    refs[-1][...] = total.astype(BF16)


def add_group(group, parts):
    part_spec = pl.BlockSpec((1, 2, 16, 16, 128), lambda n, g: (g[0], 0, 0, 0, 0))
    return pl.pallas_call(
        add_kernel,
        grid_spec=pltpu.PrefetchScalarGridSpec(
            num_scalar_prefetch=1,
            grid=(1,),
            in_specs=[part_spec] * len(parts),
            out_specs=whole(2, 16, 16, 128),
        ),
        out_shape=jax.ShapeDtypeStruct((2, 16, 16, 128), BF16),
        compiler_params=pltpu.CompilerParams(vmem_limit_bytes=VMEM_LIMIT),
        name="add_group",
    )(group, *parts)


def merge_kernel(order, *refs):
    del order
    parts, outs, stage = refs[:4], refs[4:6], refs[6]
    scale = 1.0 / math.sqrt(P_SIZE * Q * STATIONS)
    for n, part in enumerate(parts):

        @pl.when(pl.program_id(0) == n)
        def _(part=part):
            for ri in range(2):
                for i in range(16):
                    stage[ri, pl.ds(i, 16, stride=BEAM_ROWS), :] = part[ri, i].astype(F32) * scale
                for beam in range(16):
                    row = beam * BEAM_ROWS
                    outs[ri][beam] = stage[ri, row : row + 16, :]


def merge(order, parts):
    spec = pl.BlockSpec((16, 16, 128), lambda n, order: (0, order[n], 0))
    shape = jax.ShapeDtypeStruct((16, 64, 128), F32)
    return pl.pallas_call(
        merge_kernel,
        grid_spec=pltpu.PrefetchScalarGridSpec(
            num_scalar_prefetch=1,
            grid=(4,),
            in_specs=[whole(2, 16, 16, 128)] * 4,
            out_specs=[spec, spec],
            scratch_shapes=[pltpu.VMEM((2, 16 * BEAM_ROWS, 128), F32)],
        ),
        out_shape=[shape, shape],
        compiler_params=pltpu.CompilerParams(vmem_limit_bytes=VMEM_LIMIT),
        name="merge",
    )(order, *parts)


def swap_beam(value, offset):
    return lax.ppermute(value, ("yl", "c"), [(b, b ^ offset) for b in range(4)])


def station_pick(station_map):
    phys = station_map.reshape(2, 4, 32, 2).transpose(1, 3, 0, 2).reshape(STATIONS)
    return (jnp.arange(STATIONS, dtype=jnp.int32)[:, None] == phys[None, :]).astype(F32)


def pick_columns(values, pick):
    return jnp.dot(values, pick, precision=lax.Precision.HIGHEST)


def on_device(voltages, fir_taps, delays, taper, station_map, beam_order, owners):
    yh, zh, zl, x, yl, c = [lax.axis_index(name) for name in AXES]
    volts = voltages.reshape(2, 2, 75 * P_SIZE, Q).transpose(0, 2, 1, 3).reshape(2, 75, 128, Q)
    taps = fir_taps.reshape(TAPS, P_SIZE, Q)
    slots = delays.shape[1]
    stn_pos = ((yh * 4 + zh) * 2 + zl) * 4 + x
    beam_pos = yl * 2 + c
    owner = owners[beam_pos]

    pick = station_pick(station_map)
    kept = jnp.where(owner == stn_pos, delays[0], 0.0)
    model = pick_columns(kept, pick).reshape(slots, 4, 128).transpose(1, 0, 2)
    model = lax.psum_scatter(model, "zh", scatter_dimension=0, tiled=False)
    spectra = channelize(volts, taps)
    model, spectra = lax.optimization_barrier((model, spectra))
    models = lax.all_to_all(
        jnp.broadcast_to(model[None], (16, slots, 128)), ("yh", "zl", "x"), 0, 0, tiled=True
    )
    source = (owner // 32 * 2 + owner // 4 % 2) * 4 + owner % 4
    delay = lax.dynamic_index_in_dim(models, source, 0, keepdims=False)
    delay, spectra = lax.optimization_barrier((delay, spectra))
    delays_by_offset = [delay] + [swap_beam(delay, n) for n in range(1, 4)]
    turned = lax.all_to_all(spectra.reshape(64, 4, 64, 128), TURN, 0, 0, tiled=True)

    delay = jnp.stack(delays_by_offset)
    delay = jnp.where(beam_pos % 2 == 1, delay[jnp.array((1, 0, 3, 2))], delay)
    delay = jnp.where(beam_pos // 2 == 1, delay[jnp.array((2, 3, 0, 1))], delay)
    delay = delay.reshape(4 * slots, 128)
    gain = pick_columns(taper[beam_order], pick)
    gain = lax.dynamic_slice_in_dim(gain, zh * 128, 128, 1)
    first_chan = yh * 2048 + zl * 256 + x * 64 + beam_pos * 16
    unit = TWO_PI / (P_SIZE * Q)
    step = jnp.stack((jnp.cos(delay * unit), jnp.sin(delay * unit)))
    parts = []
    for dz in (2, 1, 3, 0):
        target = (zh + dz) % 4
        phase = delay * (first_chan + 512 * target).astype(F32) * unit
        base = jnp.stack((gain * jnp.cos(phase), gain * jnp.sin(phase)))
        part = form_beams(target[None], turned, base, step)
        if dz:
            part = lax.ppermute(part, "zh", [(z, (z + dz) % 4) for z in range(4)])
        parts.append(part)
    order = beam_pos ^ jnp.arange(4, dtype=jnp.int32)
    quarters = [add_group(order[n : n + 1], parts) for n in (2, 3, 1, 0)]
    quarters = [swap_beam(q, n) if n else q for q, n in zip(quarters, (2, 3, 1, 0))]
    out_re, out_im = merge(order[jnp.array((2, 3, 1, 0))], quarters)
    return (out_re, out_im)


def solution(mesh):
    torus = Mesh(mesh.devices.reshape(SIZES), AXES)
    stn, beam = AXES[:4], AXES[4:]
    return jax.shard_map(
        on_device,
        mesh=torus,
        in_specs=(P(AXES, None, None), P(), P(stn, beam, None), P(), P(), P(), P()),
        out_specs=(P(beam, stn, None), P(beam, stn, None)),
        check_vma=False,
    )
```

```python
import functools
import math

import jax
import jax.numpy as jnp
import ml_dtypes
import numpy as np
from jax import lax
from jax.experimental import pallas as pl
from jax.experimental.pallas import tpu as pltpu
from jax.sharding import Mesh
from jax.sharding import PartitionSpec as P

P_SIZE = 64
Q = 128
CHANNELS = 4096
TAPS = 12
FRAMES = 64
STATIONS = 512
TWO_PI = 2.0 * math.pi
F32 = jnp.float32
BF16 = jnp.bfloat16
VMEM_LIMIT = 56 << 20
SMALL_LIMIT = 12 << 20

AXES = ("yh", "zh", "zl", "x", "yl", "c")
SIZES = (2, 4, 2, 4, 2, 2)
TURN = ("yh", "zl", "x", "yl", "c")
FRAME_CHUNK = 16
TURN_ROWS = 132
STAGE_ROWS = 36
WIDE_ROWS = 68
BEAM_ROWS = 24


def dft_tables():
    idx = np.arange(P_SIZE)
    wide = np.arange(Q)
    first = TWO_PI / P_SIZE * (idx[:, None] * idx[None, :] % P_SIZE)
    second = TWO_PI / Q * (wide[:, None] * idx[None, :] % Q)
    twist = TWO_PI / (P_SIZE * Q) * (idx[:, None] * wide[None, :])

    def narrow(x):
        return x.astype(np.float32).astype(ml_dtypes.bfloat16)

    cos_one, sin_one = narrow(np.cos(first)), narrow(np.sin(first))
    cos_two, sin_two = narrow(np.cos(second)).T, narrow(np.sin(second)).T
    one = np.zeros((2, 2, P_SIZE, P_SIZE, 2), ml_dtypes.bfloat16)
    for pol in range(2):
        one[pol, 0, :, :, pol] = cos_one
        one[pol, 1, :, :, pol] = -sin_one
    two = np.zeros((2, P_SIZE, 2, Q), ml_dtypes.bfloat16)
    two[0, :, 0], two[0, :, 1] = cos_two, sin_two
    two[1, :, 0], two[1, :, 1] = -sin_two, cos_two
    turn = np.stack((np.cos(twist), np.sin(twist))).astype(np.float32)
    return one.reshape(4 * P_SIZE, 2 * P_SIZE), turn, two.reshape(2 * P_SIZE, 2 * Q)


def channel_kernel(
    volts, taps, one, twist, two, out, coeff_rows, folded, turned_re, turned_im, stage
):
    block = pl.program_id(1)
    for pol in range(2):
        for m in range(TAPS):
            coeff_rows[m, pl.ds(pol, 8, stride=2), :] = taps[m]
    coeff = [coeff_rows[m] for m in range(TAPS)]
    row0 = pl.multiple_of(block * 16, 16)
    for chunk in range(FRAMES // FRAME_CHUNK):
        first = chunk * FRAME_CHUNK
        window = [volts[0, first + t].astype(F32) for t in range(FRAME_CHUNK + TAPS - 1)]
        for k in range(FRAME_CHUNK):
            acc = coeff[0] * window[k]
            for m in range(1, TAPS):
                acc = acc + coeff[m] * window[k + m]
            frame = first + k
            lane = frame % 2 * Q
            folded[frame // 2, pl.ds(row0, 16), lane : lane + Q] = acc.astype(BF16)

    def first_section(pair, carry):
        part = jnp.dot(one[...], folded[pair], preferred_element_type=F32)
        for pol in range(2):
            for half in range(2):
                lanes = slice(half * Q, (half + 1) * Q)
                re = part[pol * 128 : pol * 128 + 64, lanes]
                im = part[pol * 128 + 64 : pol * 128 + 128, lanes]
                row = pol * FRAMES + pair * 2 + half
                turned_re[pl.ds(row, 64, stride=TURN_ROWS), :] = re * twist[0] + im * twist[1]
                turned_im[pl.ds(row, 64, stride=TURN_ROWS), :] = im * twist[0] - re * twist[1]
        return carry

    def second_section(j, carry):
        for i in range(16):
            row = pl.multiple_of((j * 16 + i) * TURN_ROWS, 4)
            right = jnp.concatenate(
                (
                    turned_re[pl.ds(row, 128), :].astype(BF16),
                    turned_im[pl.ds(row, 128), :].astype(BF16),
                ),
                axis=1,
            )
            part = lax.dot_general(
                two[...], right, (((1,), (1,)), ((), ())), preferred_element_type=F32
            )
            for ri in range(2):
                rows = pl.ds(ri * 16 + i, 64, stride=STAGE_ROWS)
                stage[rows, :] = part[ri * 64 : ri * 64 + 64]
        for b in range(64):
            yh, zh, zl, x = b // 32, b // 8 % 4, b // 4 % 2, b % 4
            rows = slice(b * STAGE_ROWS, b * STAGE_ROWS + 32)
            out[yh, zl, x, j, zh, 0] = stage[rows, :].astype(BF16)
        return carry

    @pl.when(block == 7)
    def _():
        lax.fori_loop(0, FRAMES // 2, first_section, 0, unroll=16)
        lax.fori_loop(0, 4, second_section, 0, unroll=4)


CHIP = pl.BlockSpec(memory_space=pltpu.VMEM)
SCALAR = pl.BlockSpec(memory_space=pltpu.SMEM)


def on_chip(value):
    return pltpu.with_memory_space_constraint(value, pltpu.VMEM)


def whole(*shape):
    return pl.BlockSpec(shape, lambda *step: (0,) * len(shape))


def channelize(volts, taps):
    one, twist, two = dft_tables()
    return pl.pallas_call(
        channel_kernel,
        grid=(2, 8),
        in_specs=[
            pl.BlockSpec((1, 75, 16, Q), lambda s, r: (s, 0, r, 0)),
            pl.BlockSpec((TAPS, 8, Q), lambda s, r: (0, r, 0)),
            whole(256, 128),
            whole(2, 64, Q),
            whole(128, 256),
        ],
        out_specs=pl.BlockSpec((2, 2, 4, 4, 4, 1, 32, 128), lambda s, r: (0, 0, 0, 0, 0, s, 0, 0)),
        out_shape=jax.ShapeDtypeStruct((2, 2, 4, 4, 4, 2, 32, 128), BF16),
        scratch_shapes=[
            pltpu.VMEM((TAPS, 16, Q), F32),
            pltpu.VMEM((FRAMES // 2, 128, 256), BF16),
            pltpu.VMEM((64 * TURN_ROWS, Q), F32),
            pltpu.VMEM((64 * TURN_ROWS, Q), F32),
            pltpu.VMEM((64 * STAGE_ROWS, 128), F32),
        ],
        compiler_params=pltpu.CompilerParams(vmem_limit_bytes=VMEM_LIMIT),
        name="channelize",
    )(volts, taps, jnp.asarray(one), jnp.asarray(twist), jnp.asarray(two))


def beam_kernel(where, spectra, base, step, out, wide):
    del where
    for src in range(64):
        wide[src * WIDE_ROWS : src * WIDE_ROWS + 64, :] = spectra[src, 0].astype(F32)
    cos_w, sin_w = base[0], base[1]
    cos_step, sin_step = step[0], step[1]
    for i in range(16):
        right = jnp.concatenate(
            [
                wide[pl.ds(s * 32 + ri * 16 + i, 64, stride=WIDE_ROWS), :].astype(BF16)
                for ri in range(2)
                for s in range(2)
            ],
            axis=0,
        )
        cos_n, sin_n = cos_w.astype(BF16), sin_w.astype(BF16)
        left = jnp.concatenate(
            (
                jnp.concatenate((cos_n, sin_n), axis=1),
                jnp.concatenate((-sin_n, cos_n), axis=1),
            ),
            axis=0,
        )
        part = jnp.dot(left, right, preferred_element_type=F32)
        for ri in range(2):
            for group in range(4):
                row = ri * 64 + group * 16
                out[group, ri, i] = part[row : row + 16].astype(BF16)
        if i < 15:
            cos_w, sin_w = (
                cos_w * cos_step - sin_w * sin_step,
                sin_w * cos_step + cos_w * sin_step,
            )


def form_beams(where, spectra, base, step):
    return pl.pallas_call(
        beam_kernel,
        grid_spec=pltpu.PrefetchScalarGridSpec(
            num_scalar_prefetch=1,
            grid=(1,),
            in_specs=[
                pl.BlockSpec((64, 1, 64, 128), lambda n, zh: (0, zh[0], 0, 0)),
                CHIP,
                CHIP,
            ],
            out_specs=CHIP,
            scratch_shapes=[pltpu.VMEM((64 * WIDE_ROWS, 128), F32)],
        ),
        out_shape=pltpu.VMEM((4, 2, 16, 16, 128), BF16),
        compiler_params=pltpu.CompilerParams(vmem_limit_bytes=SMALL_LIMIT),
        name="form_beams",
    )(where, spectra, on_chip(base), on_chip(step))


def add_kernel(offset, beam_pos, *refs):
    group = beam_pos[0] ^ offset
    total = refs[0][group].astype(F32)
    for part in refs[1:-1]:
        total = total + part[group].astype(F32)
    refs[-1][...] = total.astype(BF16)


def add_group(offset, beam_pos, parts):
    return pl.pallas_call(
        functools.partial(add_kernel, offset),
        in_specs=[SCALAR] + [CHIP] * len(parts),
        out_specs=CHIP,
        out_shape=pltpu.VMEM((2, 16, 16, 128), BF16),
        compiler_params=pltpu.CompilerParams(vmem_limit_bytes=SMALL_LIMIT),
        name="add_group",
    )(beam_pos, *[on_chip(part) for part in parts])


def merge_kernel(beam_pos, *refs):
    del beam_pos
    parts, outs, stage = refs[:4], refs[4:6], refs[6]
    scale = 1.0 / math.sqrt(P_SIZE * Q * STATIONS)
    for n, part in enumerate(parts):

        @pl.when(pl.program_id(0) == n)
        def _(part=part):
            for ri in range(2):
                for i in range(16):
                    stage[ri, pl.ds(i, 16, stride=BEAM_ROWS), :] = part[ri, i].astype(F32) * scale
                for beam in range(16):
                    row = beam * BEAM_ROWS
                    outs[ri][beam] = stage[ri, row : row + 16, :]


def merge(beam_pos, parts):
    spec = pl.BlockSpec((16, 16, 128), lambda n, pos: (0, pos[0] ^ n, 0))
    shape = jax.ShapeDtypeStruct((16, 64, 128), F32)
    return pl.pallas_call(
        merge_kernel,
        grid_spec=pltpu.PrefetchScalarGridSpec(
            num_scalar_prefetch=1,
            grid=(4,),
            in_specs=[CHIP] * 4,
            out_specs=[spec, spec],
            scratch_shapes=[pltpu.VMEM((2, 16 * BEAM_ROWS, 128), F32)],
        ),
        out_shape=[shape, shape],
        compiler_params=pltpu.CompilerParams(vmem_limit_bytes=SMALL_LIMIT),
        name="merge",
    )(beam_pos, *[on_chip(part) for part in parts])


def swap_beam(value, offset):
    return lax.ppermute(value, ("yl", "c"), [(b, b ^ offset) for b in range(4)])


def station_pick(station_map):
    phys = station_map.reshape(2, 4, 32, 2).transpose(1, 3, 0, 2).reshape(STATIONS)
    return (jnp.arange(STATIONS, dtype=jnp.int32)[:, None] == phys[None, :]).astype(F32)


def pick_columns(values, pick):
    return jnp.dot(values, pick, precision=lax.Precision.HIGHEST)


def on_device(voltages, fir_taps, delays, taper, station_map, beam_order, owners):
    yh, zh, zl, x, yl, c = [lax.axis_index(name) for name in AXES]
    volts = voltages.reshape(2, 2, 75 * P_SIZE, Q).transpose(0, 2, 1, 3).reshape(2, 75, 128, Q)
    taps = fir_taps.reshape(TAPS, P_SIZE, Q)
    slots = delays.shape[1]
    stn_pos = ((yh * 4 + zh) * 2 + zl) * 4 + x
    beam_pos = yl * 2 + c
    owner = owners[beam_pos]

    pick = station_pick(station_map)
    kept = jnp.where(owner == stn_pos, delays[0], 0.0)
    model = pick_columns(kept, pick).reshape(slots, 4, 128).transpose(1, 0, 2)
    model = lax.psum_scatter(model, "zh", scatter_dimension=0, tiled=False)
    spectra = channelize(volts, taps)
    model, spectra = lax.optimization_barrier((model, spectra))
    models = lax.all_to_all(
        jnp.broadcast_to(model[None], (16, slots, 128)), ("yh", "zl", "x"), 0, 0, tiled=True
    )
    source = (owner // 32 * 2 + owner // 4 % 2) * 4 + owner % 4
    delay = lax.dynamic_index_in_dim(models, source, 0, keepdims=False)
    delay, spectra = lax.optimization_barrier((delay, spectra))
    delays_by_offset = [delay] + [swap_beam(delay, n) for n in range(1, 4)]
    turned = lax.all_to_all(spectra.reshape(64, 4, 64, 128), TURN, 0, 0, tiled=True)

    models = delays_by_offset
    for bit in (1, 2):
        odd = beam_pos & bit != 0
        models = [jnp.where(odd, models[n ^ bit], models[n]) for n in range(4)]
    delay = jnp.concatenate(models, axis=0)
    gain = pick_columns(taper[beam_order], pick)
    gain = lax.dynamic_slice_in_dim(gain, zh * 128, 128, 1)
    first_chan = yh * 2048 + zl * 256 + x * 64 + beam_pos * 16
    unit = TWO_PI / (P_SIZE * Q)
    step = jnp.stack((jnp.cos(delay * unit), jnp.sin(delay * unit)))
    parts = []
    for dz in (2, 1, 3, 0):
        target = (zh + dz) % 4
        phase = delay * (first_chan + 512 * target).astype(F32) * unit
        base = jnp.stack((gain * jnp.cos(phase), gain * jnp.sin(phase)))
        part = form_beams(target[None], turned, base, step)
        if dz:
            part = lax.ppermute(part, "zh", [(z, (z + dz) % 4) for z in range(4)])
        parts.append(part)
    pos = beam_pos.astype(jnp.int32)[None]
    quarters = {}
    for n in (2, 3, 1, 0):
        quarter = add_group(n, pos, parts)
        quarters[n] = swap_beam(quarter, n) if n else quarter
    out_re, out_im = merge(pos, [quarters[n] for n in range(4)])
    return (out_re, out_im)


def solution(mesh):
    torus = Mesh(mesh.devices.reshape(SIZES), AXES)
    stn, beam = AXES[:4], AXES[4:]
    return jax.shard_map(
        on_device,
        mesh=torus,
        in_specs=(P(AXES, None, None), P(), P(stn, beam, None), P(), P(), P(), P()),
        out_specs=(P(beam, stn, None), P(beam, stn, None)),
        check_vma=False,
    )
```

```python
import functools
import math

import jax
import jax.numpy as jnp
import ml_dtypes
import numpy as np
from jax import lax
from jax.experimental import pallas as pl
from jax.experimental.pallas import tpu as pltpu
from jax.sharding import Mesh
from jax.sharding import PartitionSpec as P

P_SIZE = 64
Q = 128
CHANNELS = 4096
TAPS = 12
FRAMES = 64
STATIONS = 512
TWO_PI = 2.0 * math.pi
F32 = jnp.float32
BF16 = jnp.bfloat16
VMEM_LIMIT = 56 << 20
SMALL_LIMIT = 12 << 20

AXES = ("yh", "zh", "zl", "x", "yl", "c")
SIZES = (2, 4, 2, 4, 2, 2)
TURN = ("yh", "zl", "x", "yl", "c")
FRAME_CHUNK = 16
TURN_ROWS = 132
STAGE_ROWS = 36
WIDE_ROWS = 68
BEAM_ROWS = 24


def dft_tables():
    idx = np.arange(P_SIZE)
    wide = np.arange(Q)
    first = TWO_PI / P_SIZE * (idx[:, None] * idx[None, :] % P_SIZE)
    second = TWO_PI / Q * (wide[:, None] * idx[None, :] % Q)
    twist = TWO_PI / (P_SIZE * Q) * (idx[:, None] * wide[None, :])

    def narrow(x):
        return x.astype(np.float32).astype(ml_dtypes.bfloat16)

    cos_one, sin_one = narrow(np.cos(first)), narrow(np.sin(first))
    cos_two, sin_two = narrow(np.cos(second)).T, narrow(np.sin(second)).T
    one = np.zeros((2, 2, P_SIZE, P_SIZE, 2), ml_dtypes.bfloat16)
    for pol in range(2):
        one[pol, 0, :, :, pol] = cos_one
        one[pol, 1, :, :, pol] = -sin_one
    two = np.zeros((2, P_SIZE, 2, Q), ml_dtypes.bfloat16)
    two[0, :, 0], two[0, :, 1] = cos_two, sin_two
    two[1, :, 0], two[1, :, 1] = -sin_two, cos_two
    turn = np.stack((np.cos(twist), np.sin(twist))).astype(np.float32)
    return one.reshape(4 * P_SIZE, 2 * P_SIZE), turn, two.reshape(2 * P_SIZE, 2 * Q)


def channel_kernel(volts, taps, one, twist, two, *refs):
    out, coeff_rows, folded, turned_re, turned_im, stage = refs[-6:]
    block = pl.program_id(0)
    for row in range(16):
        lane = row // 2 * Q
        coeff_rows[pl.ds(row, TAPS, stride=16), :] = taps[:, lane : lane + Q]
    coeff = [coeff_rows[m * 16 : (m + 1) * 16, :] for m in range(TAPS)]
    row0 = pl.multiple_of(block * 16, 16)
    for chunk in range(FRAMES // FRAME_CHUNK):
        first = chunk * FRAME_CHUNK
        window = [volts[0, first + t].astype(F32) for t in range(FRAME_CHUNK + TAPS - 1)]
        for k in range(FRAME_CHUNK):
            acc = coeff[0] * window[k]
            for m in range(1, TAPS):
                acc = acc + coeff[m] * window[k + m]
            frame = first + k
            lane = frame % 2 * Q
            folded[frame // 2, pl.ds(row0, 16), lane : lane + Q] = acc.astype(BF16)

    def first_section(pair, carry):
        part = jnp.dot(one[...], folded[pair], preferred_element_type=F32)
        for pol in range(2):
            for half in range(2):
                lanes = slice(half * Q, (half + 1) * Q)
                re = part[pol * 128 : pol * 128 + 64, lanes]
                im = part[pol * 128 + 64 : pol * 128 + 128, lanes]
                row = pol * FRAMES + pair * 2 + half
                turned_re[pl.ds(row, 64, stride=TURN_ROWS), :] = re * twist[0] + im * twist[1]
                turned_im[pl.ds(row, 64, stride=TURN_ROWS), :] = im * twist[0] - re * twist[1]
        return carry

    def second_section(j, carry):
        for i in range(16):
            row = pl.multiple_of((j * 16 + i) * TURN_ROWS, 4)
            right = jnp.concatenate(
                (
                    turned_re[pl.ds(row, 128), :].astype(BF16),
                    turned_im[pl.ds(row, 128), :].astype(BF16),
                ),
                axis=1,
            )
            part = lax.dot_general(
                two[...], right, (((1,), (1,)), ((), ())), preferred_element_type=F32
            )
            for ri in range(2):
                rows = pl.ds(ri * 16 + i, 64, stride=STAGE_ROWS)
                stage[rows, :] = part[ri * 64 : ri * 64 + 64]
        for b in range(64):
            yh, zh, zl, x = b // 32, b // 8 % 4, b // 4 % 2, b % 4
            rows = slice(b * STAGE_ROWS, b * STAGE_ROWS + 32)
            out[yh, zl, x, j, zh, 0] = stage[rows, :].astype(BF16)
        return carry

    @pl.when(block == 7)
    def _():
        lax.fori_loop(0, FRAMES // 2, first_section, 0, unroll=16)
        lax.fori_loop(0, 4, second_section, 0, unroll=4)


CHIP = pl.BlockSpec(memory_space=pltpu.VMEM)
SCALAR = pl.BlockSpec(memory_space=pltpu.SMEM)


def on_chip(value):
    return pltpu.with_memory_space_constraint(value, pltpu.VMEM)


def whole(*shape):
    return pl.BlockSpec(shape, lambda *step: (0,) * len(shape))


def channelize(volts, taps, station, earlier=()):
    one, twist, two = dft_tables()
    return pl.pallas_call(
        channel_kernel,
        grid=(8,),
        in_specs=[
            pl.BlockSpec((1, 75, 16, Q), lambda r: (station, 0, r, 0)),
            pl.BlockSpec((TAPS, 8 * Q), lambda r: (0, r)),
            whole(256, 128),
            whole(2, 64, Q),
            whole(128, 256),
        ]
        + [pl.BlockSpec(memory_space=pl.ANY)] * len(earlier),
        out_specs=pl.BlockSpec(
            (2, 2, 4, 4, 4, 1, 32, 128), lambda r: (0, 0, 0, 0, 0, station, 0, 0)
        ),
        out_shape=jax.ShapeDtypeStruct((2, 2, 4, 4, 4, 2, 32, 128), BF16),
        input_output_aliases={5: 0} if earlier else {},
        scratch_shapes=[
            pltpu.VMEM((TAPS * 16, Q), F32),
            pltpu.VMEM((FRAMES // 2, 128, 256), BF16),
            pltpu.VMEM((64 * TURN_ROWS, Q), F32),
            pltpu.VMEM((64 * TURN_ROWS, Q), F32),
            pltpu.VMEM((64 * STAGE_ROWS, 128), F32),
        ],
        compiler_params=pltpu.CompilerParams(vmem_limit_bytes=VMEM_LIMIT),
        name="channelize",
    )(volts, taps, jnp.asarray(one), jnp.asarray(twist), jnp.asarray(two), *earlier)


def beam_kernel(where, spectra, base, step, out, wide):
    del where
    for src in range(64):
        wide[src * WIDE_ROWS : src * WIDE_ROWS + 64, :] = spectra[src, 0].astype(F32)
    cos_w, sin_w = base[0], base[1]
    cos_step, sin_step = step[0], step[1]
    for i in range(16):
        right = jnp.concatenate(
            [
                wide[pl.ds(s * 32 + ri * 16 + i, 64, stride=WIDE_ROWS), :].astype(BF16)
                for ri in range(2)
                for s in range(2)
            ],
            axis=0,
        )
        cos_n, sin_n = cos_w.astype(BF16), sin_w.astype(BF16)
        left = jnp.concatenate(
            (
                jnp.concatenate((cos_n, sin_n), axis=1),
                jnp.concatenate((-sin_n, cos_n), axis=1),
            ),
            axis=0,
        )
        part = jnp.dot(left, right, preferred_element_type=F32)
        for ri in range(2):
            for group in range(4):
                row = ri * 64 + group * 16
                out[group, ri, i] = part[row : row + 16].astype(BF16)
        if i < 15:
            cos_w, sin_w = (
                cos_w * cos_step - sin_w * sin_step,
                sin_w * cos_step + cos_w * sin_step,
            )


def form_beams(where, spectra, base, step):
    return pl.pallas_call(
        beam_kernel,
        grid_spec=pltpu.PrefetchScalarGridSpec(
            num_scalar_prefetch=1,
            grid=(1,),
            in_specs=[
                pl.BlockSpec((64, 1, 64, 128), lambda n, zh: (0, zh[0], 0, 0)),
                CHIP,
                CHIP,
            ],
            out_specs=CHIP,
            scratch_shapes=[pltpu.VMEM((64 * WIDE_ROWS, 128), F32)],
        ),
        out_shape=pltpu.VMEM((4, 2, 16, 16, 128), BF16),
        compiler_params=pltpu.CompilerParams(vmem_limit_bytes=SMALL_LIMIT),
        name="form_beams",
    )(where, spectra, on_chip(base), on_chip(step))


def add_kernel(offset, beam_pos, *refs):
    group = beam_pos[0] ^ offset
    total = refs[0][group].astype(F32)
    for part in refs[1:-1]:
        total = total + part[group].astype(F32)
    refs[-1][...] = total.astype(BF16)


def add_group(offset, beam_pos, parts):
    return pl.pallas_call(
        functools.partial(add_kernel, offset),
        in_specs=[SCALAR] + [CHIP] * len(parts),
        out_specs=CHIP,
        out_shape=pltpu.VMEM((2, 16, 16, 128), BF16),
        compiler_params=pltpu.CompilerParams(vmem_limit_bytes=SMALL_LIMIT),
        name="add_group",
    )(beam_pos, *[on_chip(part) for part in parts])


def merge_kernel(beam_pos, *refs):
    del beam_pos
    parts, outs, stage = refs[:4], refs[4:6], refs[6]
    scale = 1.0 / math.sqrt(P_SIZE * Q * STATIONS)
    for n, part in enumerate(parts):

        @pl.when(pl.program_id(0) == n)
        def _(part=part):
            for ri in range(2):
                for i in range(16):
                    stage[ri, pl.ds(i, 16, stride=BEAM_ROWS), :] = part[ri, i].astype(F32) * scale
                for beam in range(16):
                    row = beam * BEAM_ROWS
                    outs[ri][beam] = stage[ri, row : row + 16, :]


def merge(beam_pos, parts):
    spec = pl.BlockSpec((16, 16, 128), lambda n, pos: (0, pos[0] ^ n, 0))
    shape = jax.ShapeDtypeStruct((16, 64, 128), F32)
    return pl.pallas_call(
        merge_kernel,
        grid_spec=pltpu.PrefetchScalarGridSpec(
            num_scalar_prefetch=1,
            grid=(4,),
            in_specs=[CHIP] * 4,
            out_specs=[spec, spec],
            scratch_shapes=[pltpu.VMEM((2, 16 * BEAM_ROWS, 128), F32)],
        ),
        out_shape=[shape, shape],
        compiler_params=pltpu.CompilerParams(vmem_limit_bytes=SMALL_LIMIT),
        name="merge",
    )(beam_pos, *[on_chip(part) for part in parts])


def station_pick(station_map, zh):
    phys = station_map.reshape(2, 4, 32, 2).transpose(1, 3, 0, 2).reshape(STATIONS)
    phys = lax.dynamic_slice_in_dim(jnp.concatenate((phys, phys)), zh * 128, STATIONS)
    return (jnp.arange(STATIONS, dtype=jnp.int32)[:, None] == phys[None, :]).astype(F32)


def pick_columns(values, pick):
    return jnp.dot(values, pick, precision=lax.Precision.HIGHEST)


def shift(value, axis, offset):
    return lax.ppermute(value, axis, [(n, (n + offset) % 4) for n in range(4)])


def swap(value, axes, offset):
    return lax.ppermute(value, axes, [(n, n ^ offset) for n in range(4)])


def choose(index, values):
    low = jnp.where(index == 0, values[0], values[1])
    high = jnp.where(index == 2, values[2], values[3])
    return jnp.where(index < 2, low, high)


def on_device(voltages, fir_taps, delays, taper, station_map, beam_order, owners):
    yh, zh, zl, x, yl, c = [lax.axis_index(name) for name in AXES]
    volts = voltages.reshape(2, 2, 75 * P_SIZE, Q).transpose(0, 2, 1, 3).reshape(2, 75, 128, Q)
    slots = delays.shape[1]
    beam_pos = yl * 2 + c
    owner = jnp.sum(jnp.where(jnp.arange(4, dtype=jnp.int32) == beam_pos, owners, 0))
    own_yh, own_zh, own_zl, own_x = owner // 32, owner // 8 % 4, owner // 4 % 2, owner % 4

    pick = station_pick(station_map, zh)
    model = pick_columns(delays[0], pick).reshape(slots, 4, 128).transpose(1, 0, 2)
    models = [model[0]] + [shift(model[n], "zh", n) for n in range(1, 4)]
    spectra = channelize(volts, fir_taps, 0)
    *models, spectra = lax.optimization_barrier((*models, spectra))
    delay = choose((zh - own_zh) % 4, models)
    models = [delay] + [shift(delay, "x", n) for n in range(1, 4)]
    spectra = channelize(volts, fir_taps, 1, (spectra,))
    *models, spectra = lax.optimization_barrier((*models, spectra))
    delay = choose((x - own_x) % 4, models)
    models = [delay] + [swap(delay, ("yh", "zl"), n) for n in range(1, 4)]
    gain = pick_columns(taper[beam_order], pick[:, :128])
    *models, gain = lax.optimization_barrier((*models, gain))
    delay = choose((yh * 2 + zl) ^ (own_yh * 2 + own_zl), models)
    delay, spectra = lax.optimization_barrier((delay, spectra))
    models = [delay] + [swap(delay, ("yl", "c"), n) for n in range(1, 4)]
    turned = lax.all_to_all(spectra.reshape(64, 4, 64, 128), TURN, 0, 0, tiled=True)

    for bit in (1, 2):
        odd = beam_pos & bit != 0
        models = [jnp.where(odd, models[n ^ bit], models[n]) for n in range(4)]
    delay = jnp.concatenate(models, axis=0)
    first_chan = yh * 2048 + zl * 256 + x * 64 + beam_pos * 16
    unit = TWO_PI / (P_SIZE * Q)
    step = jnp.stack((jnp.cos(delay * unit), jnp.sin(delay * unit)))
    parts = []
    for dz in (2, 1, 3, 0):
        target = (zh + dz) % 4
        phase = delay * (first_chan + 512 * target).astype(F32) * unit
        base = jnp.stack((gain * jnp.cos(phase), gain * jnp.sin(phase)))
        part = form_beams(target[None], turned, base, step)
        if dz:
            part = shift(part, "zh", dz)
        parts.append(part)
    pos = beam_pos.astype(jnp.int32)[None]
    quarters = {}
    for n in (2, 3, 1, 0):
        quarter = add_group(n, pos, parts)
        quarters[n] = swap(quarter, ("yl", "c"), n) if n else quarter
    out_re, out_im = merge(pos, [quarters[n] for n in range(4)])
    return (out_re, out_im)


def solution(mesh):
    torus = Mesh(mesh.devices.reshape(SIZES), AXES)
    stn, beam = AXES[:4], AXES[4:]
    return jax.shard_map(
        on_device,
        mesh=torus,
        in_specs=(P(AXES, None, None), P(), P(stn, beam, None), P(), P(), P(), P()),
        out_specs=(P(beam, stn, None), P(beam, stn, None)),
        check_vma=False,
    )
```

```python
import functools
import math

import jax
import jax.numpy as jnp
import ml_dtypes
import numpy as np
from jax import lax
from jax.experimental import pallas as pl
from jax.experimental.pallas import tpu as pltpu
from jax.sharding import Mesh
from jax.sharding import PartitionSpec as P

P_SIZE = 64
Q = 128
CHANNELS = 4096
TAPS = 12
FRAMES = 64
STATIONS = 512
TWO_PI = 2.0 * math.pi
F32 = jnp.float32
BF16 = jnp.bfloat16
VMEM_LIMIT = 56 << 20
SMALL_LIMIT = 12 << 20

AXES = ("yh", "zh", "zl", "x", "yl", "c")
SIZES = (2, 4, 2, 4, 2, 2)
TURN = ("yh", "zl", "x", "yl", "c")
FRAME_CHUNK = 16
TURN_ROWS = 132
STAGE_ROWS = 36
WIDE_ROWS = 68
BEAM_ROWS = 24


def dft_tables():
    idx = np.arange(P_SIZE)
    wide = np.arange(Q)
    first = TWO_PI / P_SIZE * (idx[:, None] * idx[None, :] % P_SIZE)
    second = TWO_PI / Q * (wide[:, None] * idx[None, :] % Q)
    twist = TWO_PI / (P_SIZE * Q) * (idx[:, None] * wide[None, :])

    def narrow(x):
        return x.astype(np.float32).astype(ml_dtypes.bfloat16)

    cos_one, sin_one = narrow(np.cos(first)), narrow(np.sin(first))
    cos_two, sin_two = narrow(np.cos(second)).T, narrow(np.sin(second)).T
    one = np.zeros((2, 2, P_SIZE, P_SIZE, 2), ml_dtypes.bfloat16)
    for pol in range(2):
        one[pol, 0, :, :, pol] = cos_one
        one[pol, 1, :, :, pol] = -sin_one
    two = np.zeros((2, P_SIZE, 2, Q), ml_dtypes.bfloat16)
    two[0, :, 0], two[0, :, 1] = cos_two, sin_two
    two[1, :, 0], two[1, :, 1] = -sin_two, cos_two
    turn = np.stack((np.cos(twist), np.sin(twist))).astype(np.float32)
    return one.reshape(4 * P_SIZE, 2 * P_SIZE), turn, two.reshape(2 * P_SIZE, 2 * Q)


def channel_kernel(
    volts, taps, one, twist, two, out, coeff_rows, folded, turned_re, turned_im, stage
):
    block = pl.program_id(1)
    for row in range(16):
        lane = row // 2 * Q
        coeff_rows[pl.ds(row, TAPS, stride=16), :] = taps[:, lane : lane + Q]
    coeff = [coeff_rows[m * 16 : (m + 1) * 16, :] for m in range(TAPS)]
    row0 = pl.multiple_of(block * 16, 16)
    for chunk in range(FRAMES // FRAME_CHUNK):
        first = chunk * FRAME_CHUNK
        window = [volts[0, first + t].astype(F32) for t in range(FRAME_CHUNK + TAPS - 1)]
        for k in range(FRAME_CHUNK):
            acc = coeff[0] * window[k]
            for m in range(1, TAPS):
                acc = acc + coeff[m] * window[k + m]
            frame = first + k
            lane = frame % 2 * Q
            folded[frame // 2, pl.ds(row0, 16), lane : lane + Q] = acc.astype(BF16)

    def first_section(pair, carry):
        part = jnp.dot(one[...], folded[pair], preferred_element_type=F32)
        for pol in range(2):
            for half in range(2):
                lanes = slice(half * Q, (half + 1) * Q)
                re = part[pol * 128 : pol * 128 + 64, lanes]
                im = part[pol * 128 + 64 : pol * 128 + 128, lanes]
                row = pol * FRAMES + pair * 2 + half
                turned_re[pl.ds(row, 64, stride=TURN_ROWS), :] = re * twist[0] + im * twist[1]
                turned_im[pl.ds(row, 64, stride=TURN_ROWS), :] = im * twist[0] - re * twist[1]
        return carry

    def second_section(j, carry):
        for i in range(16):
            row = pl.multiple_of((j * 16 + i) * TURN_ROWS, 4)
            right = jnp.concatenate(
                (
                    turned_re[pl.ds(row, 128), :].astype(BF16),
                    turned_im[pl.ds(row, 128), :].astype(BF16),
                ),
                axis=1,
            )
            part = lax.dot_general(
                two[...], right, (((1,), (1,)), ((), ())), preferred_element_type=F32
            )
            for ri in range(2):
                rows = pl.ds(ri * 16 + i, 64, stride=STAGE_ROWS)
                stage[rows, :] = part[ri * 64 : ri * 64 + 64]
        for b in range(64):
            yh, zh, zl, x = b // 32, b // 8 % 4, b // 4 % 2, b % 4
            rows = slice(b * STAGE_ROWS, b * STAGE_ROWS + 32)
            out[yh, zl, x, j, zh, 0] = stage[rows, :].astype(BF16)
        return carry

    @pl.when(block == 7)
    def _():
        lax.fori_loop(0, FRAMES // 2, first_section, 0, unroll=16)
        lax.fori_loop(0, 4, second_section, 0, unroll=4)


CHIP = pl.BlockSpec(memory_space=pltpu.VMEM)
SCALAR = pl.BlockSpec(memory_space=pltpu.SMEM)


def on_chip(value):
    return pltpu.with_memory_space_constraint(value, pltpu.VMEM)


def whole(*shape):
    return pl.BlockSpec(shape, lambda *step: (0,) * len(shape))


def channelize(volts, taps):
    one, twist, two = dft_tables()
    return pl.pallas_call(
        channel_kernel,
        grid=(2, 8),
        in_specs=[
            pl.BlockSpec((1, 75, 16, Q), lambda s, r: (s, 0, r, 0)),
            pl.BlockSpec((TAPS, 8 * Q), lambda s, r: (0, r)),
            whole(256, 128),
            whole(2, 64, Q),
            whole(128, 256),
        ],
        out_specs=pl.BlockSpec((2, 2, 4, 4, 4, 1, 32, 128), lambda s, r: (0, 0, 0, 0, 0, s, 0, 0)),
        out_shape=jax.ShapeDtypeStruct((2, 2, 4, 4, 4, 2, 32, 128), BF16),
        scratch_shapes=[
            pltpu.VMEM((TAPS * 16, Q), F32),
            pltpu.VMEM((FRAMES // 2, 128, 256), BF16),
            pltpu.VMEM((64 * TURN_ROWS, Q), F32),
            pltpu.VMEM((64 * TURN_ROWS, Q), F32),
            pltpu.VMEM((64 * STAGE_ROWS, 128), F32),
        ],
        compiler_params=pltpu.CompilerParams(vmem_limit_bytes=VMEM_LIMIT),
        name="channelize",
    )(volts, taps, jnp.asarray(one), jnp.asarray(twist), jnp.asarray(two))


def beam_kernel(where, spectra, base, step, out_re, out_im, wide):
    del where
    for src in range(64):
        wide[src * WIDE_ROWS : src * WIDE_ROWS + 64, :] = spectra[src, 0].astype(F32)
    cos_w, sin_w = base[0], base[1]
    cos_step, sin_step = step[0], step[1]
    for i in range(16):
        right = jnp.concatenate(
            [
                wide[pl.ds(s * 32 + ri * 16 + i, 64, stride=WIDE_ROWS), :].astype(BF16)
                for ri in range(2)
                for s in range(2)
            ],
            axis=0,
        )
        cos_n, sin_n = cos_w.astype(BF16), sin_w.astype(BF16)
        left = jnp.concatenate(
            (
                jnp.concatenate((cos_n, sin_n), axis=1),
                jnp.concatenate((-sin_n, cos_n), axis=1),
            ),
            axis=0,
        )
        part = jnp.dot(left, right, preferred_element_type=F32)
        for ri, out in enumerate((out_re, out_im)):
            for group in range(4):
                row = ri * 64 + group * 16
                out[group, i] = part[row : row + 16].astype(BF16)
        if i < 15:
            cos_w, sin_w = (
                cos_w * cos_step - sin_w * sin_step,
                sin_w * cos_step + cos_w * sin_step,
            )


def form_beams(where, spectra, base, step):
    return pl.pallas_call(
        beam_kernel,
        grid_spec=pltpu.PrefetchScalarGridSpec(
            num_scalar_prefetch=1,
            grid=(1,),
            in_specs=[
                pl.BlockSpec((64, 1, 64, 128), lambda n, zh: (0, zh[0], 0, 0)),
                CHIP,
                CHIP,
            ],
            out_specs=[CHIP, CHIP],
            scratch_shapes=[pltpu.VMEM((64 * WIDE_ROWS, 128), F32)],
        ),
        out_shape=[pltpu.VMEM((4, 16, 16, 128), BF16)] * 2,
        compiler_params=pltpu.CompilerParams(vmem_limit_bytes=SMALL_LIMIT),
        name="form_beams",
    )(where, spectra, on_chip(base), on_chip(step))


def add_pair_kernel(one, other, out):
    for group in range(4):
        out[group] = (one[group].astype(F32) + other[group].astype(F32)).astype(BF16)


def add_pair(one, other):
    return pl.pallas_call(
        add_pair_kernel,
        in_specs=[CHIP, CHIP],
        out_specs=CHIP,
        out_shape=pltpu.VMEM((4, 16, 16, 128), BF16),
        compiler_params=pltpu.CompilerParams(vmem_limit_bytes=SMALL_LIMIT),
        name="add_pair",
    )(on_chip(one), on_chip(other))


def add_kernel(offset, beam_pos, *refs):
    group = beam_pos[0] ^ offset
    parts, out = refs[:-1], refs[-1]
    for ri in range(2):
        total = parts[ri][group].astype(F32)
        for part in parts[2 + ri :: 2]:
            total = total + part[group].astype(F32)
        out[ri] = total.astype(BF16)


def add_group(offset, beam_pos, parts):
    flat = [on_chip(value) for pair in parts for value in pair]
    return pl.pallas_call(
        functools.partial(add_kernel, offset),
        in_specs=[SCALAR] + [CHIP] * len(flat),
        out_specs=CHIP,
        out_shape=pltpu.VMEM((2, 16, 16, 128), BF16),
        compiler_params=pltpu.CompilerParams(vmem_limit_bytes=SMALL_LIMIT),
        name="add_group",
    )(beam_pos, *flat)


def merge_kernel(beam_pos, *refs):
    del beam_pos
    parts, outs, stage = refs[:4], refs[4:6], refs[6]
    scale = 1.0 / math.sqrt(P_SIZE * Q * STATIONS)
    for n, part in enumerate(parts):

        @pl.when(pl.program_id(0) == n)
        def _(part=part):
            for ri in range(2):
                for i in range(16):
                    stage[ri, pl.ds(i, 16, stride=BEAM_ROWS), :] = part[ri, i].astype(F32) * scale
                for beam in range(16):
                    row = beam * BEAM_ROWS
                    outs[ri][beam] = stage[ri, row : row + 16, :]


def merge(beam_pos, parts):
    spec = pl.BlockSpec((16, 16, 128), lambda n, pos: (0, pos[0] ^ n, 0))
    shape = jax.ShapeDtypeStruct((16, 64, 128), F32)
    return pl.pallas_call(
        merge_kernel,
        grid_spec=pltpu.PrefetchScalarGridSpec(
            num_scalar_prefetch=1,
            grid=(4,),
            in_specs=[CHIP] * 4,
            out_specs=[spec, spec],
            scratch_shapes=[pltpu.VMEM((2, 16 * BEAM_ROWS, 128), F32)],
        ),
        out_shape=[shape, shape],
        compiler_params=pltpu.CompilerParams(vmem_limit_bytes=SMALL_LIMIT),
        name="merge",
    )(beam_pos, *[on_chip(part) for part in parts])


def station_pick(station_map):
    phys = station_map.reshape(2, 4, 32, 2).transpose(1, 3, 0, 2).reshape(STATIONS)
    return (jnp.arange(STATIONS, dtype=jnp.int32)[:, None] == phys[None, :]).astype(F32)


def pick_columns(values, pick):
    return jnp.dot(values, pick, precision=lax.Precision.HIGHEST)


def shift(value, axis, offset):
    return lax.ppermute(value, axis, [(n, (n + offset) % 4) for n in range(4)])


def swap(value, axes, offset):
    return lax.ppermute(value, axes, [(n, n ^ offset) for n in range(4)])


def on_device(voltages, fir_taps, delays, taper, station_map, beam_order, owners):
    yh, zh, zl, x, yl, c = [lax.axis_index(name) for name in AXES]
    volts = voltages.reshape(2, 2, 75 * P_SIZE, Q).transpose(0, 2, 1, 3).reshape(2, 75, 128, Q)
    slots = delays.shape[1]
    beam_pos = yl * 2 + c

    pick = station_pick(station_map)
    model = pick_columns(delays[0], pick).reshape(slots, 4, 128).transpose(1, 0, 2)
    model = jnp.broadcast_to(model[None, :, None], (2, 4, 8, slots, 128))
    models = lax.all_to_all(model.reshape(64, slots, 128), AXES[:4], 0, 0, tiled=True)
    spectra = channelize(volts, fir_taps)
    models, spectra = lax.optimization_barrier((models, spectra))
    delay = lax.dynamic_index_in_dim(models, owners[beam_pos], 0, keepdims=False)
    delay, spectra = lax.optimization_barrier((delay, spectra))
    models = [delay] + [swap(delay, ("yl", "c"), n) for n in range(1, 4)]
    turned = lax.all_to_all(spectra.reshape(64, 4, 64, 128), TURN, 0, 0, tiled=True)

    for bit in (1, 2):
        odd = beam_pos & bit != 0
        models = [jnp.where(odd, models[n ^ bit], models[n]) for n in range(4)]
    delay = jnp.concatenate(models, axis=0)
    gain = pick_columns(taper[beam_order], pick)
    gain = lax.dynamic_slice_in_dim(gain, zh * 128, 128, 1)
    first_chan = yh * 2048 + zl * 256 + x * 64 + beam_pos * 16
    unit = TWO_PI / (P_SIZE * Q)
    step = jnp.stack((jnp.cos(delay * unit), jnp.sin(delay * unit)))

    def beams_for(offset):
        target = (zh + offset) % 4
        phase = delay * (first_chan + 512 * target).astype(F32) * unit
        base = jnp.stack((gain * jnp.cos(phase), gain * jnp.sin(phase)))
        return form_beams(target[None], turned, base, step)

    far_re, far_im = beams_for(2)
    far_re, far_im = shift(far_re, "zh", 1), shift(far_im, "zh", 3)
    up_re, up_im = beams_for(1)
    up_im = shift(up_im, "zh", 1)
    down_re, down_im = beams_for(3)
    down_re = shift(down_re, "zh", 3)
    own = beams_for(0)
    up_re = shift(add_pair(up_re, far_re), "zh", 1)
    down_im = shift(add_pair(down_im, far_im), "zh", 3)
    parts = [own, (up_re, up_im), (down_re, down_im)]
    pos = beam_pos.astype(jnp.int32)[None]
    quarters = {}
    for n in (2, 3, 1, 0):
        quarter = add_group(n, pos, parts)
        quarters[n] = swap(quarter, ("yl", "c"), n) if n else quarter
    out_re, out_im = merge(pos, [quarters[n] for n in range(4)])
    return (out_re, out_im)


def solution(mesh):
    torus = Mesh(mesh.devices.reshape(SIZES), AXES)
    stn, beam = AXES[:4], AXES[4:]
    return jax.shard_map(
        on_device,
        mesh=torus,
        in_specs=(P(AXES, None, None), P(), P(stn, beam, None), P(), P(), P(), P()),
        out_specs=(P(beam, stn, None), P(beam, stn, None)),
        check_vma=False,
    )
```

```python
import functools
import math

import jax
import jax.numpy as jnp
import ml_dtypes
import numpy as np
from jax import lax
from jax.experimental import pallas as pl
from jax.experimental.pallas import tpu as pltpu
from jax.sharding import Mesh
from jax.sharding import PartitionSpec as P

P_SIZE = 64
Q = 128
CHANNELS = 4096
TAPS = 12
FRAMES = 64
STATIONS = 512
TWO_PI = 2.0 * math.pi
F32 = jnp.float32
BF16 = jnp.bfloat16
VMEM_LIMIT = 56 << 20
SMALL_LIMIT = 12 << 20

AXES = ("yh", "zh", "zl", "x", "yl", "c")
SIZES = (2, 4, 2, 4, 2, 2)
TURN = ("yh", "zl", "x", "yl", "c")
FRAME_CHUNK = 16
TURN_ROWS = 132
STAGE_ROWS = 36
WIDE_ROWS = 68
BEAM_ROWS = 24


def dft_tables():
    idx = np.arange(P_SIZE)
    wide = np.arange(Q)
    first = TWO_PI / P_SIZE * (idx[:, None] * idx[None, :] % P_SIZE)
    second = TWO_PI / Q * (wide[:, None] * idx[None, :] % Q)
    twist = TWO_PI / (P_SIZE * Q) * (idx[:, None] * wide[None, :])

    def narrow(x):
        return x.astype(np.float32).astype(ml_dtypes.bfloat16)

    cos_one, sin_one = narrow(np.cos(first)), narrow(np.sin(first))
    cos_two, sin_two = narrow(np.cos(second)).T, narrow(np.sin(second)).T
    one = np.zeros((2, 2, P_SIZE, P_SIZE, 2), ml_dtypes.bfloat16)
    for pol in range(2):
        one[pol, 0, :, :, pol] = cos_one
        one[pol, 1, :, :, pol] = -sin_one
    two = np.zeros((2, P_SIZE, 2, Q), ml_dtypes.bfloat16)
    two[0, :, 0], two[0, :, 1] = cos_two, sin_two
    two[1, :, 0], two[1, :, 1] = -sin_two, cos_two
    turn = np.stack((np.cos(twist), np.sin(twist))).astype(np.float32)
    return one.reshape(4 * P_SIZE, 2 * P_SIZE), turn, two.reshape(2 * P_SIZE, 2 * Q)


def channel_kernel(
    volts, taps, one, twist, two, out, coeff_rows, folded, turned_re, turned_im, stage
):
    block = pl.program_id(1)
    for row in range(16):
        lane = row // 2 * Q
        coeff_rows[pl.ds(row, TAPS, stride=16), :] = taps[:, lane : lane + Q]
    coeff = [coeff_rows[m * 16 : (m + 1) * 16, :] for m in range(TAPS)]
    row0 = pl.multiple_of(block * 16, 16)
    for chunk in range(FRAMES // FRAME_CHUNK):
        first = chunk * FRAME_CHUNK
        window = [volts[0, first + t].astype(F32) for t in range(FRAME_CHUNK + TAPS - 1)]
        for k in range(FRAME_CHUNK):
            acc = coeff[0] * window[k]
            for m in range(1, TAPS):
                acc = acc + coeff[m] * window[k + m]
            frame = first + k
            lane = frame % 2 * Q
            folded[frame // 2, pl.ds(row0, 16), lane : lane + Q] = acc.astype(BF16)

    def first_section(pair, carry):
        part = jnp.dot(one[...], folded[pair], preferred_element_type=F32)
        for pol in range(2):
            for half in range(2):
                lanes = slice(half * Q, (half + 1) * Q)
                re = part[pol * 128 : pol * 128 + 64, lanes]
                im = part[pol * 128 + 64 : pol * 128 + 128, lanes]
                row = pol * FRAMES + pair * 2 + half
                turned_re[pl.ds(row, 64, stride=TURN_ROWS), :] = re * twist[0] + im * twist[1]
                turned_im[pl.ds(row, 64, stride=TURN_ROWS), :] = im * twist[0] - re * twist[1]
        return carry

    def second_section(j, carry):
        for i in range(16):
            row = pl.multiple_of((j * 16 + i) * TURN_ROWS, 4)
            right = jnp.concatenate(
                (
                    turned_re[pl.ds(row, 128), :].astype(BF16),
                    turned_im[pl.ds(row, 128), :].astype(BF16),
                ),
                axis=1,
            )
            part = lax.dot_general(
                two[...], right, (((1,), (1,)), ((), ())), preferred_element_type=F32
            )
            for ri in range(2):
                rows = pl.ds(ri * 16 + i, 64, stride=STAGE_ROWS)
                stage[rows, :] = part[ri * 64 : ri * 64 + 64]
        for b in range(64):
            yh, zh, zl, x = b // 32, b // 8 % 4, b // 4 % 2, b % 4
            rows = slice(b * STAGE_ROWS, b * STAGE_ROWS + 32)
            out[yh, zl, x, j, zh, 0] = stage[rows, :].astype(BF16)
        return carry

    @pl.when(block == 7)
    def _():
        lax.fori_loop(0, FRAMES // 2, first_section, 0, unroll=32)
        lax.fori_loop(0, 4, second_section, 0, unroll=4)


CHIP = pl.BlockSpec(memory_space=pltpu.VMEM)
SCALAR = pl.BlockSpec(memory_space=pltpu.SMEM)


def on_chip(value):
    return pltpu.with_memory_space_constraint(value, pltpu.VMEM)


def whole(*shape):
    return pl.BlockSpec(shape, lambda *step: (0,) * len(shape))


def channelize(volts, taps):
    one, twist, two = dft_tables()
    return pl.pallas_call(
        channel_kernel,
        grid=(2, 8),
        in_specs=[
            pl.BlockSpec((1, 75, 16, Q), lambda s, r: (s, 0, r, 0)),
            pl.BlockSpec((TAPS, 8 * Q), lambda s, r: (0, r)),
            whole(256, 128),
            whole(2, 64, Q),
            whole(128, 256),
        ],
        out_specs=pl.BlockSpec((2, 2, 4, 4, 4, 1, 32, 128), lambda s, r: (0, 0, 0, 0, 0, s, 0, 0)),
        out_shape=jax.ShapeDtypeStruct((2, 2, 4, 4, 4, 2, 32, 128), BF16),
        scratch_shapes=[
            pltpu.VMEM((TAPS * 16, Q), F32),
            pltpu.VMEM((FRAMES // 2, 128, 256), BF16),
            pltpu.VMEM((64 * TURN_ROWS, Q), F32),
            pltpu.VMEM((64 * TURN_ROWS, Q), F32),
            pltpu.VMEM((64 * STAGE_ROWS, 128), F32),
        ],
        compiler_params=pltpu.CompilerParams(vmem_limit_bytes=VMEM_LIMIT),
        name="channelize",
    )(volts, taps, jnp.asarray(one), jnp.asarray(twist), jnp.asarray(two))


def beam_kernel(where, spectra, base, step, out_re, out_im, wide):
    del where
    for src in range(64):
        wide[src * WIDE_ROWS : src * WIDE_ROWS + 64, :] = spectra[src, 0].astype(F32)
    cos_w, sin_w = base[0], base[1]
    cos_step, sin_step = step[0], step[1]
    for i in range(16):
        right = jnp.concatenate(
            [
                wide[pl.ds(s * 32 + ri * 16 + i, 64, stride=WIDE_ROWS), :].astype(BF16)
                for ri in range(2)
                for s in range(2)
            ],
            axis=0,
        )
        cos_n, sin_n = cos_w.astype(BF16), sin_w.astype(BF16)
        left = jnp.concatenate(
            (
                jnp.concatenate((cos_n, sin_n), axis=1),
                jnp.concatenate((-sin_n, cos_n), axis=1),
            ),
            axis=0,
        )
        part = jnp.dot(left, right, preferred_element_type=F32)
        for ri, out in enumerate((out_re, out_im)):
            for group in range(4):
                row = ri * 64 + group * 16
                out[group, i] = part[row : row + 16].astype(BF16)
        if i < 15:
            cos_w, sin_w = (
                cos_w * cos_step - sin_w * sin_step,
                sin_w * cos_step + cos_w * sin_step,
            )


def form_beams(where, spectra, base, step):
    return pl.pallas_call(
        beam_kernel,
        grid_spec=pltpu.PrefetchScalarGridSpec(
            num_scalar_prefetch=1,
            grid=(1,),
            in_specs=[
                pl.BlockSpec((64, 1, 64, 128), lambda n, zh: (0, zh[0], 0, 0)),
                CHIP,
                CHIP,
            ],
            out_specs=[CHIP, CHIP],
            scratch_shapes=[pltpu.VMEM((64 * WIDE_ROWS, 128), F32)],
        ),
        out_shape=[pltpu.VMEM((4, 16, 16, 128), BF16)] * 2,
        compiler_params=pltpu.CompilerParams(vmem_limit_bytes=SMALL_LIMIT),
        name="form_beams",
    )(where, spectra, on_chip(base), on_chip(step))


def add_pair_kernel(one, other, out):
    for group in range(4):
        out[group] = (one[group].astype(F32) + other[group].astype(F32)).astype(BF16)


def add_pair(one, other):
    return pl.pallas_call(
        add_pair_kernel,
        in_specs=[CHIP, CHIP],
        out_specs=CHIP,
        out_shape=pltpu.VMEM((4, 16, 16, 128), BF16),
        compiler_params=pltpu.CompilerParams(vmem_limit_bytes=SMALL_LIMIT),
        name="add_pair",
    )(on_chip(one), on_chip(other))


def add_kernel(offset, beam_pos, *refs):
    group = beam_pos[0] ^ offset
    parts, out = refs[:-1], refs[-1]
    for ri in range(2):
        total = parts[ri][group].astype(F32)
        for part in parts[2 + ri :: 2]:
            total = total + part[group].astype(F32)
        out[ri] = total.astype(BF16)


def add_group(offset, beam_pos, parts):
    flat = [on_chip(value) for pair in parts for value in pair]
    return pl.pallas_call(
        functools.partial(add_kernel, offset),
        in_specs=[SCALAR] + [CHIP] * len(flat),
        out_specs=CHIP,
        out_shape=pltpu.VMEM((2, 16, 16, 128), BF16),
        compiler_params=pltpu.CompilerParams(vmem_limit_bytes=SMALL_LIMIT),
        name="add_group",
    )(beam_pos, *flat)


def merge_kernel(beam_pos, *refs):
    del beam_pos
    parts, outs, stage = refs[:4], refs[4:6], refs[6]
    scale = 1.0 / math.sqrt(P_SIZE * Q * STATIONS)
    for n, part in enumerate(parts):

        @pl.when(pl.program_id(0) == n)
        def _(part=part):
            for ri in range(2):
                for i in range(16):
                    stage[ri, pl.ds(i, 16, stride=BEAM_ROWS), :] = part[ri, i].astype(F32) * scale
                for beam in range(16):
                    row = beam * BEAM_ROWS
                    outs[ri][beam] = stage[ri, row : row + 16, :]


def merge(beam_pos, parts):
    spec = pl.BlockSpec((16, 16, 128), lambda n, pos: (0, pos[0] ^ n, 0))
    shape = jax.ShapeDtypeStruct((16, 64, 128), F32)
    return pl.pallas_call(
        merge_kernel,
        grid_spec=pltpu.PrefetchScalarGridSpec(
            num_scalar_prefetch=1,
            grid=(4,),
            in_specs=[CHIP] * 4,
            out_specs=[spec, spec],
            scratch_shapes=[pltpu.VMEM((2, 16 * BEAM_ROWS, 128), F32)],
        ),
        out_shape=[shape, shape],
        compiler_params=pltpu.CompilerParams(vmem_limit_bytes=SMALL_LIMIT),
        name="merge",
    )(beam_pos, *[on_chip(part) for part in parts])


def keep_kernel(beam_pos, owners, models, out):
    out[...] = models[owners[beam_pos[0]]]


def keep_owner(beam_pos, owners, models):
    return pl.pallas_call(
        keep_kernel,
        in_specs=[SCALAR, SCALAR, CHIP],
        out_specs=CHIP,
        out_shape=pltpu.VMEM(models.shape[1:], F32),
        compiler_params=pltpu.CompilerParams(vmem_limit_bytes=SMALL_LIMIT),
        name="keep_owner",
    )(beam_pos, owners, on_chip(models))


def station_pick(station_map):
    phys = station_map.reshape(2, 4, 32, 2).transpose(1, 3, 0, 2).reshape(STATIONS)
    return (jnp.arange(STATIONS, dtype=jnp.int32)[:, None] == phys[None, :]).astype(F32)


def pick_columns(values, pick):
    return jnp.dot(values, pick, precision=lax.Precision.HIGHEST)


def shift(value, axis, offset):
    return lax.ppermute(value, axis, [(n, (n + offset) % 4) for n in range(4)])


def swap(value, axes, offset):
    return lax.ppermute(value, axes, [(n, n ^ offset) for n in range(4)])


def on_device(voltages, fir_taps, delays, taper, station_map, beam_order, owners):
    yh, zh, zl, x, yl, c = [lax.axis_index(name) for name in AXES]
    volts = voltages.reshape(2, 2, 75 * P_SIZE, Q).transpose(0, 2, 1, 3).reshape(2, 75, 128, Q)
    slots = delays.shape[1]
    beam_pos = yl * 2 + c

    pick = station_pick(station_map)
    model = pick_columns(delays[0], pick).reshape(slots, 4, 128).transpose(1, 0, 2)
    model = jnp.broadcast_to(model[None, :, None], (2, 4, 8, slots, 128))
    models = lax.all_to_all(model.reshape(64, slots, 128), AXES[:4], 0, 0, tiled=True)
    spectra = channelize(volts, fir_taps)
    models, spectra = lax.optimization_barrier((models, spectra))
    pos = beam_pos.astype(jnp.int32)[None]
    delay = keep_owner(pos, owners, models)
    delay, spectra = lax.optimization_barrier((delay, spectra))
    models = [delay] + [swap(delay, ("yl", "c"), n) for n in range(1, 4)]
    turned = lax.all_to_all(spectra.reshape(64, 4, 64, 128), TURN, 0, 0, tiled=True)

    for bit in (1, 2):
        odd = beam_pos & bit != 0
        models = [jnp.where(odd, models[n ^ bit], models[n]) for n in range(4)]
    delay = jnp.concatenate(models, axis=0)
    gain = pick_columns(taper[beam_order], pick)
    gain = lax.dynamic_slice_in_dim(gain, zh * 128, 128, 1)
    first_chan = yh * 2048 + zl * 256 + x * 64 + beam_pos * 16
    unit = TWO_PI / (P_SIZE * Q)
    step = jnp.stack((jnp.cos(delay * unit), jnp.sin(delay * unit)))

    def beams_for(offset):
        target = (zh + offset) % 4
        phase = delay * (first_chan + 512 * target).astype(F32) * unit
        base = jnp.stack((gain * jnp.cos(phase), gain * jnp.sin(phase)))
        return form_beams(target[None], turned, base, step)

    far_re, far_im = beams_for(2)
    far_re, far_im = shift(far_re, "zh", 1), shift(far_im, "zh", 3)
    up_re, up_im = beams_for(1)
    up_im = shift(up_im, "zh", 1)
    down_re, down_im = beams_for(3)
    down_re = shift(down_re, "zh", 3)
    own = beams_for(0)
    up_re = shift(add_pair(up_re, far_re), "zh", 1)
    down_im = shift(add_pair(down_im, far_im), "zh", 3)
    parts = [own, (up_re, up_im), (down_re, down_im)]
    quarters = {}
    for n in (2, 3, 1, 0):
        quarter = add_group(n, pos, parts)
        quarters[n] = swap(quarter, ("yl", "c"), n) if n else quarter
    out_re, out_im = merge(pos, [quarters[n] for n in range(4)])
    return (out_re, out_im)


def solution(mesh):
    torus = Mesh(mesh.devices.reshape(SIZES), AXES)
    stn, beam = AXES[:4], AXES[4:]
    return jax.shard_map(
        on_device,
        mesh=torus,
        in_specs=(P(AXES, None, None), P(), P(stn, beam, None), P(), P(), P(), P()),
        out_specs=(P(beam, stn, None), P(beam, stn, None)),
        check_vma=False,
    )
```

```python
import functools
import math

import jax
import jax.numpy as jnp
import ml_dtypes
import numpy as np
from jax import lax
from jax.experimental import pallas as pl
from jax.experimental.pallas import tpu as pltpu
from jax.sharding import Mesh
from jax.sharding import PartitionSpec as P

P_SIZE = 64
Q = 128
CHANNELS = 4096
TAPS = 12
FRAMES = 64
STATIONS = 512
TWO_PI = 2.0 * math.pi
F32 = jnp.float32
BF16 = jnp.bfloat16
VMEM_LIMIT = 56 << 20
SMALL_LIMIT = 12 << 20

AXES = ("yh", "zh", "zl", "x", "yl", "c")
SIZES = (2, 4, 2, 4, 2, 2)
TURN = ("yh", "zl", "x", "yl", "c")
FRAME_CHUNK = 16
TURN_ROWS = 132
STAGE_ROWS = 36
WIDE_ROWS = 68
BEAM_ROWS = 24


def dft_tables():
    idx = np.arange(P_SIZE)
    wide = np.arange(Q)
    first = TWO_PI / P_SIZE * (idx[:, None] * idx[None, :] % P_SIZE)
    second = TWO_PI / Q * (wide[:, None] * idx[None, :] % Q)
    twist = TWO_PI / (P_SIZE * Q) * (idx[:, None] * wide[None, :])

    def narrow(x):
        return x.astype(np.float32).astype(ml_dtypes.bfloat16)

    cos_one, sin_one = narrow(np.cos(first)), narrow(np.sin(first))
    cos_two, sin_two = narrow(np.cos(second)).T, narrow(np.sin(second)).T
    one = np.zeros((2, 2, P_SIZE, P_SIZE, 2), ml_dtypes.bfloat16)
    for pol in range(2):
        one[pol, 0, :, :, pol] = cos_one
        one[pol, 1, :, :, pol] = -sin_one
    two = np.zeros((2, P_SIZE, 2, Q), ml_dtypes.bfloat16)
    two[0, :, 0], two[0, :, 1] = cos_two, sin_two
    two[1, :, 0], two[1, :, 1] = -sin_two, cos_two
    turn = np.stack((np.cos(twist), np.sin(twist))).astype(np.float32)
    return one.reshape(4 * P_SIZE, 2 * P_SIZE), turn, two.reshape(2 * P_SIZE, 2 * Q)


def channel_kernel(
    volts, taps, one, twist, two, out, coeff_rows, folded, turned_re, turned_im, stage
):
    block = pl.program_id(1)
    for row in range(16):
        lane = row // 2 * Q
        coeff_rows[pl.ds(row, TAPS, stride=16), :] = taps[:, lane : lane + Q]
    coeff = [coeff_rows[m * 16 : (m + 1) * 16, :] for m in range(TAPS)]
    row0 = pl.multiple_of(block * 16, 16)
    for chunk in range(FRAMES // FRAME_CHUNK):
        first = chunk * FRAME_CHUNK
        window = [volts[0, first + t].astype(F32) for t in range(FRAME_CHUNK + TAPS - 1)]
        for k in range(FRAME_CHUNK):
            acc = coeff[0] * window[k]
            for m in range(1, TAPS):
                acc = acc + coeff[m] * window[k + m]
            frame = first + k
            lane = frame % 2 * Q
            folded[frame // 2, pl.ds(row0, 16), lane : lane + Q] = acc.astype(BF16)

    def first_section(pair, carry):
        part = jnp.dot(one[...], folded[pair], preferred_element_type=F32)
        for pol in range(2):
            for half in range(2):
                lanes = slice(half * Q, (half + 1) * Q)
                re = part[pol * 128 : pol * 128 + 64, lanes]
                im = part[pol * 128 + 64 : pol * 128 + 128, lanes]
                row = pol * FRAMES + pair * 2 + half
                turned_re[pl.ds(row, 64, stride=TURN_ROWS), :] = re * twist[0] + im * twist[1]
                turned_im[pl.ds(row, 64, stride=TURN_ROWS), :] = im * twist[0] - re * twist[1]
        return carry

    def second_section(j, carry):
        for i in range(16):
            row = pl.multiple_of((j * 16 + i) * TURN_ROWS, 4)
            right = jnp.concatenate(
                (
                    turned_re[pl.ds(row, 128), :].astype(BF16),
                    turned_im[pl.ds(row, 128), :].astype(BF16),
                ),
                axis=1,
            )
            part = lax.dot_general(
                two[...], right, (((1,), (1,)), ((), ())), preferred_element_type=F32
            )
            for ri in range(2):
                rows = pl.ds(ri * 16 + i, 64, stride=STAGE_ROWS)
                stage[rows, :] = part[ri * 64 : ri * 64 + 64]
        for b in range(64):
            yh, zh, zl, x = b // 32, b // 8 % 4, b // 4 % 2, b % 4
            rows = slice(b * STAGE_ROWS, b * STAGE_ROWS + 32)
            out[yh, zl, x, j, zh, 0] = stage[rows, :].astype(BF16)
        return carry

    @pl.when(block == 7)
    def _():
        lax.fori_loop(0, FRAMES // 2, first_section, 0, unroll=32)
        lax.fori_loop(0, 4, second_section, 0, unroll=4)


CHIP = pl.BlockSpec(memory_space=pltpu.VMEM)
SCALAR = pl.BlockSpec(memory_space=pltpu.SMEM)


def on_chip(value):
    return pltpu.with_memory_space_constraint(value, pltpu.VMEM)


def whole(*shape):
    return pl.BlockSpec(shape, lambda *step: (0,) * len(shape))


def channelize(volts, taps):
    one, twist, two = dft_tables()
    return pl.pallas_call(
        channel_kernel,
        grid=(2, 8),
        in_specs=[
            pl.BlockSpec((1, 75, 16, Q), lambda s, r: (s, 0, r, 0)),
            pl.BlockSpec((TAPS, 8 * Q), lambda s, r: (0, r)),
            whole(256, 128),
            whole(2, 64, Q),
            whole(128, 256),
        ],
        out_specs=pl.BlockSpec((2, 2, 4, 4, 4, 1, 32, 128), lambda s, r: (0, 0, 0, 0, 0, s, 0, 0)),
        out_shape=jax.ShapeDtypeStruct((2, 2, 4, 4, 4, 2, 32, 128), BF16),
        scratch_shapes=[
            pltpu.VMEM((TAPS * 16, Q), F32),
            pltpu.VMEM((FRAMES // 2, 128, 256), BF16),
            pltpu.VMEM((64 * TURN_ROWS, Q), F32),
            pltpu.VMEM((64 * TURN_ROWS, Q), F32),
            pltpu.VMEM((64 * STAGE_ROWS, 128), F32),
        ],
        compiler_params=pltpu.CompilerParams(vmem_limit_bytes=VMEM_LIMIT),
        name="channelize",
    )(volts, taps, jnp.asarray(one), jnp.asarray(twist), jnp.asarray(two))


def beam_kernel(where, spectra, base, step, out_re, out_im, wide):
    del where
    for src in range(64):
        wide[src * WIDE_ROWS : src * WIDE_ROWS + 64, :] = spectra[src, 0].astype(F32)
    cos_w, sin_w = base[0], base[1]
    cos_step, sin_step = step[0], step[1]
    for i in range(16):
        right = jnp.concatenate(
            [
                wide[pl.ds(s * 32 + ri * 16 + i, 64, stride=WIDE_ROWS), :].astype(BF16)
                for ri in range(2)
                for s in range(2)
            ],
            axis=0,
        )
        cos_n, sin_n = cos_w.astype(BF16), sin_w.astype(BF16)
        left = jnp.concatenate(
            (
                jnp.concatenate((cos_n, sin_n), axis=1),
                jnp.concatenate((-sin_n, cos_n), axis=1),
            ),
            axis=0,
        )
        part = jnp.dot(left, right, preferred_element_type=F32)
        for ri, out in enumerate((out_re, out_im)):
            for group in range(4):
                row = ri * 64 + group * 16
                out[group, i] = part[row : row + 16].astype(BF16)
        if i < 15:
            cos_w, sin_w = (
                cos_w * cos_step - sin_w * sin_step,
                sin_w * cos_step + cos_w * sin_step,
            )


def form_beams(where, spectra, base, step):
    return pl.pallas_call(
        beam_kernel,
        grid_spec=pltpu.PrefetchScalarGridSpec(
            num_scalar_prefetch=1,
            grid=(1,),
            in_specs=[
                pl.BlockSpec((64, 1, 64, 128), lambda n, zh: (0, zh[0], 0, 0)),
                CHIP,
                CHIP,
            ],
            out_specs=[CHIP, CHIP],
            scratch_shapes=[pltpu.VMEM((64 * WIDE_ROWS, 128), F32)],
        ),
        out_shape=[pltpu.VMEM((4, 16, 16, 128), BF16)] * 2,
        compiler_params=pltpu.CompilerParams(vmem_limit_bytes=SMALL_LIMIT),
        name="form_beams",
    )(where, spectra, on_chip(base), on_chip(step))


def add_pair_kernel(one, other, out):
    for group in range(4):
        out[group] = (one[group].astype(F32) + other[group].astype(F32)).astype(BF16)


def add_pair(one, other):
    return pl.pallas_call(
        add_pair_kernel,
        in_specs=[CHIP, CHIP],
        out_specs=CHIP,
        out_shape=pltpu.VMEM((4, 16, 16, 128), BF16),
        compiler_params=pltpu.CompilerParams(vmem_limit_bytes=SMALL_LIMIT),
        name="add_pair",
    )(on_chip(one), on_chip(other))


def add_kernel(offset, beam_pos, *refs):
    group = beam_pos[0] ^ offset
    total = refs[0][group].astype(F32)
    for part in refs[1:-1]:
        total = total + part[group].astype(F32)
    refs[-1][...] = total.astype(BF16)


def add_group(offset, beam_pos, parts):
    return pl.pallas_call(
        functools.partial(add_kernel, offset),
        in_specs=[SCALAR] + [CHIP] * len(parts),
        out_specs=CHIP,
        out_shape=pltpu.VMEM((16, 16, 128), BF16),
        compiler_params=pltpu.CompilerParams(vmem_limit_bytes=SMALL_LIMIT),
        name="add_group",
    )(beam_pos, *[on_chip(part) for part in parts])


def merge_kernel(beam_pos, *refs):
    del beam_pos
    parts, out, stage = refs[:4], refs[4], refs[5]
    scale = 1.0 / math.sqrt(P_SIZE * Q * STATIONS)
    for n, part in enumerate(parts):

        @pl.when(pl.program_id(0) == n)
        def _(part=part):
            for i in range(16):
                stage[pl.ds(i, 16, stride=BEAM_ROWS), :] = part[i].astype(F32) * scale
            for beam in range(16):
                row = beam * BEAM_ROWS
                out[beam] = stage[row : row + 16, :]


def merge(beam_pos, parts):
    return pl.pallas_call(
        merge_kernel,
        grid_spec=pltpu.PrefetchScalarGridSpec(
            num_scalar_prefetch=1,
            grid=(4,),
            in_specs=[CHIP] * 4,
            out_specs=pl.BlockSpec((16, 16, 128), lambda n, pos: (0, pos[0] ^ n, 0)),
            scratch_shapes=[pltpu.VMEM((16 * BEAM_ROWS, 128), F32)],
        ),
        out_shape=jax.ShapeDtypeStruct((16, 64, 128), F32),
        compiler_params=pltpu.CompilerParams(vmem_limit_bytes=SMALL_LIMIT),
        name="merge",
    )(beam_pos, *[on_chip(part) for part in parts])


def keep_kernel(beam_pos, owners, models, out):
    out[...] = models[owners[beam_pos[0]]]


def keep_owner(beam_pos, owners, models):
    return pl.pallas_call(
        keep_kernel,
        in_specs=[SCALAR, SCALAR, CHIP],
        out_specs=CHIP,
        out_shape=pltpu.VMEM(models.shape[1:], F32),
        compiler_params=pltpu.CompilerParams(vmem_limit_bytes=SMALL_LIMIT),
        name="keep_owner",
    )(beam_pos, owners, on_chip(models))


def station_pick(station_map):
    phys = station_map.reshape(2, 4, 32, 2).transpose(1, 3, 0, 2).reshape(STATIONS)
    return (jnp.arange(STATIONS, dtype=jnp.int32)[:, None] == phys[None, :]).astype(F32)


def pick_columns(values, pick):
    return jnp.dot(values, pick, precision=lax.Precision.HIGHEST)


def shift(value, axis, offset):
    return lax.ppermute(value, axis, [(n, (n + offset) % 4) for n in range(4)])


def swap(value, axes, offset):
    return lax.ppermute(value, axes, [(n, n ^ offset) for n in range(4)])


def on_device(voltages, fir_taps, delays, taper, station_map, beam_order, owners):
    yh, zh, zl, x, yl, c = [lax.axis_index(name) for name in AXES]
    volts = voltages.reshape(2, 2, 75 * P_SIZE, Q).transpose(0, 2, 1, 3).reshape(2, 75, 128, Q)
    slots = delays.shape[1]
    beam_pos = yl * 2 + c

    pick = station_pick(station_map)
    model = pick_columns(delays[0], pick).reshape(slots, 4, 128).transpose(1, 0, 2)
    model = jnp.broadcast_to(model[None, :, None], (2, 4, 8, slots, 128))
    models = lax.all_to_all(model.reshape(64, slots, 128), AXES[:4], 0, 0, tiled=True)
    spectra = channelize(volts, fir_taps)
    models, spectra = lax.optimization_barrier((models, spectra))
    pos = beam_pos.astype(jnp.int32)[None]
    delay = keep_owner(pos, owners, models)
    delay, spectra = lax.optimization_barrier((delay, spectra))
    models = [delay] + [swap(delay, ("yl", "c"), n) for n in range(1, 4)]
    turned = lax.all_to_all(spectra.reshape(64, 4, 64, 128), TURN, 0, 0, tiled=True)

    for bit in (1, 2):
        odd = beam_pos & bit != 0
        models = [jnp.where(odd, models[n ^ bit], models[n]) for n in range(4)]
    delay = jnp.concatenate(models, axis=0)
    gain = pick_columns(taper[beam_order], pick)
    gain = lax.dynamic_slice_in_dim(gain, zh * 128, 128, 1)
    first_chan = yh * 2048 + zl * 256 + x * 64 + beam_pos * 16
    unit = TWO_PI / (P_SIZE * Q)
    step = jnp.stack((jnp.cos(delay * unit), jnp.sin(delay * unit)))

    def beams_for(offset):
        target = (zh + offset) % 4
        phase = delay * (first_chan + 512 * target).astype(F32) * unit
        base = jnp.stack((gain * jnp.cos(phase), gain * jnp.sin(phase)))
        return form_beams(target[None], turned, base, step)

    far_re, far_im = beams_for(2)
    far_re, far_im = shift(far_re, "zh", 1), shift(far_im, "zh", 3)
    up_re, up_im = beams_for(1)
    up_im = shift(up_im, "zh", 1)
    down_re, down_im = beams_for(3)
    down_re = shift(down_re, "zh", 3)
    own = beams_for(0)
    up_re = shift(add_pair(up_re, far_re), "zh", 1)
    down_im = shift(add_pair(down_im, far_im), "zh", 3)
    outs = []
    for parts in ((own[0], up_re, down_re), (own[1], up_im, down_im)):
        quarters = {}
        for n in (2, 3, 1, 0):
            quarter = add_group(n, pos, parts)
            quarters[n] = swap(quarter, ("yl", "c"), n) if n else quarter
        outs.append([quarters[n] for n in range(4)])
    return tuple(merge(pos, quarters) for quarters in outs)


def solution(mesh):
    torus = Mesh(mesh.devices.reshape(SIZES), AXES)
    stn, beam = AXES[:4], AXES[4:]
    return jax.shard_map(
        on_device,
        mesh=torus,
        in_specs=(P(AXES, None, None), P(), P(stn, beam, None), P(), P(), P(), P()),
        out_specs=(P(beam, stn, None), P(beam, stn, None)),
        check_vma=False,
    )
```

```python
import functools
import math

import jax
import jax.numpy as jnp
import ml_dtypes
import numpy as np
from jax import lax
from jax.experimental import pallas as pl
from jax.experimental.pallas import tpu as pltpu
from jax.sharding import Mesh
from jax.sharding import PartitionSpec as P

P_SIZE = 64
Q = 128
CHANNELS = 4096
TAPS = 12
FRAMES = 64
STATIONS = 512
TWO_PI = 2.0 * math.pi
F32 = jnp.float32
BF16 = jnp.bfloat16
VMEM_LIMIT = 56 << 20
SMALL_LIMIT = 12 << 20

AXES = ("yh", "zh", "zl", "x", "yl", "c")
SIZES = (2, 4, 2, 4, 2, 2)
TURN = ("yh", "zl", "x", "yl", "c")
FRAME_CHUNK = 16
TURN_ROWS = 132
STAGE_ROWS = 36
WIDE_ROWS = 34
BEAM_ROWS = 24


def dft_tables():
    idx = np.arange(P_SIZE)
    wide = np.arange(Q)
    first = TWO_PI / P_SIZE * (idx[:, None] * idx[None, :] % P_SIZE)
    second = TWO_PI / Q * (wide[:, None] * idx[None, :] % Q)
    twist = TWO_PI / (P_SIZE * Q) * (idx[:, None] * wide[None, :])

    def narrow(x):
        return x.astype(np.float32).astype(ml_dtypes.bfloat16)

    cos_one, sin_one = narrow(np.cos(first)), narrow(np.sin(first))
    cos_two, sin_two = narrow(np.cos(second)).T, narrow(np.sin(second)).T
    one = np.zeros((2, 2, P_SIZE, P_SIZE, 2), ml_dtypes.bfloat16)
    for pol in range(2):
        one[pol, 0, :, :, pol] = cos_one
        one[pol, 1, :, :, pol] = -sin_one
    two = np.zeros((2, P_SIZE, 2, Q), ml_dtypes.bfloat16)
    two[0, :, 0], two[0, :, 1] = cos_two, sin_two
    two[1, :, 0], two[1, :, 1] = -sin_two, cos_two
    turn = np.stack((np.cos(twist), np.sin(twist))).astype(np.float32)
    return one.reshape(4 * P_SIZE, 2 * P_SIZE), turn, two.reshape(2 * P_SIZE, 2 * Q)


def channel_kernel(
    volts, taps, one, twist, two, out, coeff_rows, folded, turned_re, turned_im, stage
):
    block = pl.program_id(1)
    for row in range(16):
        lane = row // 2 * Q
        coeff_rows[pl.ds(row, TAPS, stride=16), :] = taps[:, lane : lane + Q]
    coeff = [coeff_rows[m * 16 : (m + 1) * 16, :] for m in range(TAPS)]
    row0 = pl.multiple_of(block * 16, 16)
    for chunk in range(FRAMES // FRAME_CHUNK):
        first = chunk * FRAME_CHUNK
        window = [volts[0, first + t].astype(F32) for t in range(FRAME_CHUNK + TAPS - 1)]
        for k in range(FRAME_CHUNK):
            acc = coeff[0] * window[k]
            for m in range(1, TAPS):
                acc = acc + coeff[m] * window[k + m]
            frame = first + k
            lane = frame % 2 * Q
            folded[frame // 2, pl.ds(row0, 16), lane : lane + Q] = acc.astype(BF16)

    def first_section(pair, carry):
        part = jnp.dot(one[...], folded[pair], preferred_element_type=F32)
        for pol in range(2):
            for half in range(2):
                lanes = slice(half * Q, (half + 1) * Q)
                re = part[pol * 128 : pol * 128 + 64, lanes]
                im = part[pol * 128 + 64 : pol * 128 + 128, lanes]
                row = pol * FRAMES + pair * 2 + half
                turned_re[pl.ds(row, 64, stride=TURN_ROWS), :] = re * twist[0] + im * twist[1]
                turned_im[pl.ds(row, 64, stride=TURN_ROWS), :] = im * twist[0] - re * twist[1]
        return carry

    def second_section(j, carry):
        for i in range(16):
            row = pl.multiple_of((j * 16 + i) * TURN_ROWS, 4)
            right = jnp.concatenate(
                (
                    turned_re[pl.ds(row, 128), :].astype(BF16),
                    turned_im[pl.ds(row, 128), :].astype(BF16),
                ),
                axis=1,
            )
            part = lax.dot_general(
                two[...], right, (((1,), (1,)), ((), ())), preferred_element_type=F32
            )
            for ri in range(2):
                rows = pl.ds(ri * 16 + i, 64, stride=STAGE_ROWS)
                stage[rows, :] = part[ri * 64 : ri * 64 + 64]
        for b in range(64):
            yh, zh, zl, x = b // 32, b // 8 % 4, b // 4 % 2, b % 4
            rows = slice(b * STAGE_ROWS, b * STAGE_ROWS + 32)
            out[yh, zl, x, j, zh, 0] = stage[rows, :].astype(BF16)
        return carry

    @pl.when(block == 7)
    def _():
        lax.fori_loop(0, FRAMES // 2, first_section, 0, unroll=32)
        lax.fori_loop(0, 4, second_section, 0, unroll=4)


CHIP = pl.BlockSpec(memory_space=pltpu.VMEM)
SCALAR = pl.BlockSpec(memory_space=pltpu.SMEM)


def on_chip(value):
    return pltpu.with_memory_space_constraint(value, pltpu.VMEM)


def whole(*shape):
    return pl.BlockSpec(shape, lambda *step: (0,) * len(shape))


def channelize(volts, taps):
    one, twist, two = dft_tables()
    return pl.pallas_call(
        channel_kernel,
        grid=(2, 8),
        in_specs=[
            pl.BlockSpec((1, 75, 16, Q), lambda s, r: (s, 0, r, 0)),
            pl.BlockSpec((TAPS, 8 * Q), lambda s, r: (0, r)),
            whole(256, 128),
            whole(2, 64, Q),
            whole(128, 256),
        ],
        out_specs=pl.BlockSpec((2, 2, 4, 4, 4, 1, 32, 128), lambda s, r: (0, 0, 0, 0, 0, s, 0, 0)),
        out_shape=jax.ShapeDtypeStruct((2, 2, 4, 4, 4, 2, 32, 128), BF16),
        scratch_shapes=[
            pltpu.VMEM((TAPS * 16, Q), F32),
            pltpu.VMEM((FRAMES // 2, 128, 256), BF16),
            pltpu.VMEM((64 * TURN_ROWS, Q), F32),
            pltpu.VMEM((64 * TURN_ROWS, Q), F32),
            pltpu.VMEM((64 * STAGE_ROWS, 128), F32),
        ],
        compiler_params=pltpu.CompilerParams(vmem_limit_bytes=VMEM_LIMIT),
        name="channelize",
    )(volts, taps, jnp.asarray(one), jnp.asarray(twist), jnp.asarray(two))


def beam_kernel(where, spectra, base, step, out_re, out_im, wide):
    del where
    for src in range(64):
        for s in range(2):
            row = (src * 2 + s) * WIDE_ROWS
            wide[row : row + 32, :] = spectra[src, 0, s * 32 : s * 32 + 32, :].astype(F32)
    cos_w, sin_w = base[0], base[1]
    cos_step, sin_step = step[0], step[1]
    for i in range(16):
        right = jnp.concatenate(
            [
                wide[pl.ds(ri * 16 + i, 128, stride=WIDE_ROWS), :].astype(BF16)
                for ri in range(2)
            ],
            axis=0,
        )
        cos_n, sin_n = cos_w.astype(BF16), sin_w.astype(BF16)
        left = jnp.concatenate(
            (
                jnp.concatenate((cos_n, sin_n), axis=1),
                jnp.concatenate((-sin_n, cos_n), axis=1),
            ),
            axis=0,
        )
        part = jnp.dot(left, right, preferred_element_type=F32)
        for ri, out in enumerate((out_re, out_im)):
            for group in range(4):
                row = ri * 64 + group * 16
                out[group, i] = part[row : row + 16].astype(BF16)
        if i < 15:
            cos_w, sin_w = (
                cos_w * cos_step - sin_w * sin_step,
                sin_w * cos_step + cos_w * sin_step,
            )


def form_beams(where, spectra, base, step):
    return pl.pallas_call(
        beam_kernel,
        grid_spec=pltpu.PrefetchScalarGridSpec(
            num_scalar_prefetch=1,
            grid=(1,),
            in_specs=[
                pl.BlockSpec((64, 1, 64, 128), lambda n, zh: (0, zh[0], 0, 0)),
                CHIP,
                CHIP,
            ],
            out_specs=[CHIP, CHIP],
            scratch_shapes=[pltpu.VMEM((128 * WIDE_ROWS, 128), F32)],
        ),
        out_shape=[pltpu.VMEM((4, 16, 16, 128), BF16)] * 2,
        compiler_params=pltpu.CompilerParams(vmem_limit_bytes=SMALL_LIMIT),
        name="form_beams",
    )(where, spectra, on_chip(base), on_chip(step))


def add_pair_kernel(one, other, out):
    for group in range(4):
        out[group] = (one[group].astype(F32) + other[group].astype(F32)).astype(BF16)


def add_pair(one, other):
    return pl.pallas_call(
        add_pair_kernel,
        in_specs=[CHIP, CHIP],
        out_specs=CHIP,
        out_shape=pltpu.VMEM((4, 16, 16, 128), BF16),
        compiler_params=pltpu.CompilerParams(vmem_limit_bytes=SMALL_LIMIT),
        name="add_pair",
    )(on_chip(one), on_chip(other))


def add_kernel(offset, beam_pos, *refs):
    group = beam_pos[0] ^ offset
    total = refs[0][group].astype(F32)
    for part in refs[1:-1]:
        total = total + part[group].astype(F32)
    refs[-1][...] = total.astype(BF16)


def add_group(offset, beam_pos, parts):
    return pl.pallas_call(
        functools.partial(add_kernel, offset),
        in_specs=[SCALAR] + [CHIP] * len(parts),
        out_specs=CHIP,
        out_shape=pltpu.VMEM((16, 16, 128), BF16),
        compiler_params=pltpu.CompilerParams(vmem_limit_bytes=SMALL_LIMIT),
        name="add_group",
    )(beam_pos, *[on_chip(part) for part in parts])


def merge_kernel(beam_pos, *refs):
    del beam_pos
    parts, out, stage = refs[:4], refs[4], refs[5]
    scale = 1.0 / math.sqrt(P_SIZE * Q * STATIONS)
    for n, part in enumerate(parts):

        @pl.when(pl.program_id(0) == n)
        def _(part=part):
            for i in range(16):
                stage[pl.ds(i, 16, stride=BEAM_ROWS), :] = part[i].astype(F32) * scale
            for beam in range(16):
                row = beam * BEAM_ROWS
                out[beam] = stage[row : row + 16, :]


def merge(beam_pos, parts):
    return pl.pallas_call(
        merge_kernel,
        grid_spec=pltpu.PrefetchScalarGridSpec(
            num_scalar_prefetch=1,
            grid=(4,),
            in_specs=[CHIP] * 4,
            out_specs=pl.BlockSpec((16, 16, 128), lambda n, pos: (0, pos[0] ^ n, 0)),
            scratch_shapes=[pltpu.VMEM((16 * BEAM_ROWS, 128), F32)],
        ),
        out_shape=jax.ShapeDtypeStruct((16, 64, 128), F32),
        compiler_params=pltpu.CompilerParams(vmem_limit_bytes=SMALL_LIMIT),
        name="merge",
    )(beam_pos, *[on_chip(part) for part in parts])


def keep_kernel(beam_pos, owners, models, out):
    out[...] = models[owners[beam_pos[0]]]


def keep_owner(beam_pos, owners, models):
    return pl.pallas_call(
        keep_kernel,
        in_specs=[SCALAR, SCALAR, CHIP],
        out_specs=CHIP,
        out_shape=pltpu.VMEM(models.shape[1:], F32),
        compiler_params=pltpu.CompilerParams(vmem_limit_bytes=SMALL_LIMIT),
        name="keep_owner",
    )(beam_pos, owners, on_chip(models))


def station_pick(station_map):
    starts = [(yh * 4 + zh) * 64 for zh in range(4) for yh in range(2)]
    phys = jnp.concatenate([station_map[n : n + 64] for n in starts])
    return (jnp.arange(STATIONS, dtype=jnp.int32)[:, None] == phys[None, :]).astype(F32)


def pick_columns(values, pick):
    return jnp.dot(values, pick, precision=lax.Precision.HIGHEST)


def shift(value, axis, offset):
    return lax.ppermute(value, axis, [(n, (n + offset) % 4) for n in range(4)])


def swap(value, axes, offset):
    return lax.ppermute(value, axes, [(n, n ^ offset) for n in range(4)])


def on_device(voltages, fir_taps, delays, taper, station_map, beam_order, owners):
    yh, zh, zl, x, yl, c = [lax.axis_index(name) for name in AXES]
    volts = voltages.reshape(2, 2, 75 * P_SIZE, Q).transpose(0, 2, 1, 3).reshape(2, 75, 128, Q)
    slots = delays.shape[1]
    beam_pos = yl * 2 + c

    pick = station_pick(station_map)
    model = pick_columns(delays[0], pick).reshape(slots, 4, 128).transpose(1, 0, 2)
    model = jnp.broadcast_to(model[None, :, None], (2, 4, 8, slots, 128))
    models = lax.all_to_all(model.reshape(64, slots, 128), AXES[:4], 0, 0, tiled=True)
    spectra = channelize(volts, fir_taps)
    models, spectra = lax.optimization_barrier((models, spectra))
    pos = beam_pos.astype(jnp.int32)[None]
    delay = keep_owner(pos, owners, models)
    delay, spectra = lax.optimization_barrier((delay, spectra))
    models = [delay] + [swap(delay, ("yl", "c"), n) for n in range(1, 4)]
    turned = lax.all_to_all(spectra.reshape(64, 4, 64, 128), TURN, 0, 0, tiled=True)

    for bit in (1, 2):
        odd = beam_pos & bit != 0
        models = [jnp.where(odd, models[n ^ bit], models[n]) for n in range(4)]
    delay = jnp.concatenate(models, axis=0)
    gain = pick_columns(taper[beam_order], pick)
    gain = lax.dynamic_slice_in_dim(gain, zh * 128, 128, 1)
    first_chan = yh * 2048 + zl * 256 + x * 64 + beam_pos * 16
    unit = TWO_PI / (P_SIZE * Q)
    step = jnp.stack((jnp.cos(delay * unit), jnp.sin(delay * unit)))

    def beams_for(offset):
        target = (zh + offset) % 4
        phase = delay * (first_chan + 512 * target).astype(F32) * unit
        base = jnp.stack((gain * jnp.cos(phase), gain * jnp.sin(phase)))
        return form_beams(target[None], turned, base, step)

    far_re, far_im = beams_for(2)
    far_re, far_im = shift(far_re, "zh", 1), shift(far_im, "zh", 3)
    up_re, up_im = beams_for(1)
    up_im = shift(up_im, "zh", 1)
    down_re, down_im = beams_for(3)
    down_re = shift(down_re, "zh", 3)
    own = beams_for(0)
    up_re = shift(add_pair(up_re, far_re), "zh", 1)
    down_im = shift(add_pair(down_im, far_im), "zh", 3)
    outs = []
    for parts in ((own[0], up_re, down_re), (own[1], up_im, down_im)):
        quarters = {}
        for n in (2, 3, 1, 0):
            quarter = add_group(n, pos, parts)
            quarters[n] = swap(quarter, ("yl", "c"), n) if n else quarter
        outs.append([quarters[n] for n in range(4)])
    return tuple(merge(pos, quarters) for quarters in outs)


def solution(mesh):
    torus = Mesh(mesh.devices.reshape(SIZES), AXES)
    stn, beam = AXES[:4], AXES[4:]
    return jax.shard_map(
        on_device,
        mesh=torus,
        in_specs=(P(AXES, None, None), P(), P(stn, beam, None), P(), P(), P(), P()),
        out_specs=(P(beam, stn, None), P(beam, stn, None)),
        check_vma=False,
    )
```

```python
import functools
import math

import jax
import jax.numpy as jnp
import ml_dtypes
import numpy as np
from jax import lax
from jax.experimental import pallas as pl
from jax.experimental.pallas import tpu as pltpu
from jax.sharding import Mesh
from jax.sharding import PartitionSpec as P

P_SIZE = 64
Q = 128
CHANNELS = 4096
TAPS = 12
FRAMES = 64
STATIONS = 512
TWO_PI = 2.0 * math.pi
F32 = jnp.float32
BF16 = jnp.bfloat16
VMEM_LIMIT = 56 << 20
SMALL_LIMIT = 12 << 20

AXES = ("yh", "zh", "zl", "x", "yl", "c")
SIZES = (2, 4, 2, 4, 2, 2)
TURN = ("yh", "zl", "x", "yl", "c")
FRAME_CHUNK = 16
TURN_ROWS = 132
STAGE_ROWS = 36
WIDE_ROWS = 34
BEAM_ROWS = 24


def dft_tables():
    idx = np.arange(P_SIZE)
    wide = np.arange(Q)
    first = TWO_PI / P_SIZE * (idx[:, None] * idx[None, :] % P_SIZE)
    second = TWO_PI / Q * (wide[:, None] * idx[None, :] % Q)
    twist = TWO_PI / (P_SIZE * Q) * (idx[:, None] * wide[None, :])

    def narrow(x):
        return x.astype(np.float32).astype(ml_dtypes.bfloat16)

    cos_one, sin_one = narrow(np.cos(first)), narrow(np.sin(first))
    cos_two, sin_two = narrow(np.cos(second)).T, narrow(np.sin(second)).T
    one = np.zeros((2, 2, P_SIZE, P_SIZE, 2), ml_dtypes.bfloat16)
    for pol in range(2):
        one[pol, 0, :, :, pol] = cos_one
        one[pol, 1, :, :, pol] = -sin_one
    two = np.zeros((2, P_SIZE, 2, Q), ml_dtypes.bfloat16)
    two[0, :, 0], two[0, :, 1] = cos_two, sin_two
    two[1, :, 0], two[1, :, 1] = -sin_two, cos_two
    turn = np.stack((np.cos(twist), np.sin(twist))).astype(np.float32)
    return one.reshape(4 * P_SIZE, 2 * P_SIZE), turn, two.reshape(2 * P_SIZE, 2 * Q)


def channel_kernel(
    volts, taps, one, twist, two, out, coeff_rows, folded, turned_re, turned_im, stage
):
    block = pl.program_id(1)
    for row in range(16):
        lane = row // 2 * Q
        coeff_rows[pl.ds(row, TAPS, stride=16), :] = taps[:, lane : lane + Q]
    coeff = [coeff_rows[m * 16 : (m + 1) * 16, :] for m in range(TAPS)]
    row0 = pl.multiple_of(block * 16, 16)
    for chunk in range(FRAMES // FRAME_CHUNK):
        first = chunk * FRAME_CHUNK
        window = [volts[0, first + t].astype(F32) for t in range(FRAME_CHUNK + TAPS - 1)]
        for k in range(FRAME_CHUNK):
            acc = coeff[0] * window[k]
            for m in range(1, TAPS):
                acc = acc + coeff[m] * window[k + m]
            frame = first + k
            lane = frame % 2 * Q
            folded[frame // 2, pl.ds(row0, 16), lane : lane + Q] = acc.astype(BF16)

    def first_section(pair, carry):
        part = jnp.dot(one[...], folded[pair], preferred_element_type=F32)
        for pol in range(2):
            for half in range(2):
                lanes = slice(half * Q, (half + 1) * Q)
                re = part[pol * 128 : pol * 128 + 64, lanes]
                im = part[pol * 128 + 64 : pol * 128 + 128, lanes]
                row = pol * FRAMES + pair * 2 + half
                turned_re[pl.ds(row, 64, stride=TURN_ROWS), :] = re * twist[0] + im * twist[1]
                turned_im[pl.ds(row, 64, stride=TURN_ROWS), :] = im * twist[0] - re * twist[1]
        return carry

    def second_section(j, carry):
        for i in range(16):
            row = pl.multiple_of((j * 16 + i) * TURN_ROWS, 4)
            right = jnp.concatenate(
                (
                    turned_re[pl.ds(row, 128), :].astype(BF16),
                    turned_im[pl.ds(row, 128), :].astype(BF16),
                ),
                axis=1,
            )
            part = lax.dot_general(
                two[...], right, (((1,), (1,)), ((), ())), preferred_element_type=F32
            )
            for ri in range(2):
                rows = pl.ds(ri * 16 + i, 64, stride=STAGE_ROWS)
                stage[rows, :] = part[ri * 64 : ri * 64 + 64]
        for b in range(64):
            yh, zh, zl, x = b // 32, b // 8 % 4, b // 4 % 2, b % 4
            rows = slice(b * STAGE_ROWS, b * STAGE_ROWS + 32)
            out[yh, zl, x, j, zh, 0] = stage[rows, :].astype(BF16)
        return carry

    @pl.when(block == 7)
    def _():
        lax.fori_loop(0, FRAMES // 2, first_section, 0, unroll=32)
        lax.fori_loop(0, 4, second_section, 0, unroll=4)


CHIP = pl.BlockSpec(memory_space=pltpu.VMEM)
SCALAR = pl.BlockSpec(memory_space=pltpu.SMEM)


def on_chip(value):
    return pltpu.with_memory_space_constraint(value, pltpu.VMEM)


def whole(*shape):
    return pl.BlockSpec(shape, lambda *step: (0,) * len(shape))


def channelize(volts, taps):
    one, twist, two = dft_tables()
    return pl.pallas_call(
        channel_kernel,
        grid=(2, 8),
        in_specs=[
            pl.BlockSpec((1, 75, 16, Q), lambda s, r: (s, 0, r, 0)),
            pl.BlockSpec((TAPS, 8 * Q), lambda s, r: (0, r)),
            CHIP,
            CHIP,
            CHIP,
        ],
        out_specs=pl.BlockSpec((2, 2, 4, 4, 4, 1, 32, 128), lambda s, r: (0, 0, 0, 0, 0, s, 0, 0)),
        out_shape=jax.ShapeDtypeStruct((2, 2, 4, 4, 4, 2, 32, 128), BF16),
        scratch_shapes=[
            pltpu.VMEM((TAPS * 16, Q), F32),
            pltpu.VMEM((FRAMES // 2, 128, 256), BF16),
            pltpu.VMEM((64 * TURN_ROWS, Q), F32),
            pltpu.VMEM((64 * TURN_ROWS, Q), F32),
            pltpu.VMEM((64 * STAGE_ROWS, 128), F32),
        ],
        compiler_params=pltpu.CompilerParams(vmem_limit_bytes=VMEM_LIMIT),
        name="channelize",
    )(volts, taps, *[on_chip(jnp.asarray(table)) for table in (one, twist, two)])


def beam_kernel(where, spectra, base, step, out_re, out_im, wide):
    del where
    for src in range(64):
        for s in range(2):
            row = (src * 2 + s) * WIDE_ROWS
            wide[row : row + 32, :] = spectra[src, 0, s * 32 : s * 32 + 32, :].astype(F32)
    cos_w, sin_w = base[0], base[1]
    cos_step, sin_step = step[0], step[1]
    for i in range(16):
        right = jnp.concatenate(
            [
                wide[pl.ds(ri * 16 + i, 128, stride=WIDE_ROWS), :].astype(BF16)
                for ri in range(2)
            ],
            axis=0,
        )
        cos_n, sin_n = cos_w.astype(BF16), sin_w.astype(BF16)
        left = jnp.concatenate(
            (
                jnp.concatenate((cos_n, sin_n), axis=1),
                jnp.concatenate((-sin_n, cos_n), axis=1),
            ),
            axis=0,
        )
        part = jnp.dot(left, right, preferred_element_type=F32)
        for ri, out in enumerate((out_re, out_im)):
            for group in range(4):
                row = ri * 64 + group * 16
                out[group, i] = part[row : row + 16].astype(BF16)
        if i < 15:
            cos_w, sin_w = (
                cos_w * cos_step - sin_w * sin_step,
                sin_w * cos_step + cos_w * sin_step,
            )


def form_beams(where, spectra, base, step):
    return pl.pallas_call(
        beam_kernel,
        grid_spec=pltpu.PrefetchScalarGridSpec(
            num_scalar_prefetch=1,
            grid=(1,),
            in_specs=[
                pl.BlockSpec((64, 1, 64, 128), lambda n, zh: (0, zh[0], 0, 0)),
                CHIP,
                CHIP,
            ],
            out_specs=[CHIP, CHIP],
            scratch_shapes=[pltpu.VMEM((128 * WIDE_ROWS, 128), F32)],
        ),
        out_shape=[pltpu.VMEM((4, 16, 16, 128), BF16)] * 2,
        compiler_params=pltpu.CompilerParams(vmem_limit_bytes=SMALL_LIMIT),
        name="form_beams",
    )(where, spectra, on_chip(base), on_chip(step))


def add_pair_kernel(one, other, out):
    for group in range(4):
        out[group] = (one[group].astype(F32) + other[group].astype(F32)).astype(BF16)


def add_pair(one, other):
    return pl.pallas_call(
        add_pair_kernel,
        in_specs=[CHIP, CHIP],
        out_specs=CHIP,
        out_shape=pltpu.VMEM((4, 16, 16, 128), BF16),
        compiler_params=pltpu.CompilerParams(vmem_limit_bytes=SMALL_LIMIT),
        name="add_pair",
    )(on_chip(one), on_chip(other))


def add_kernel(offset, beam_pos, *refs):
    group = beam_pos[0] ^ offset
    total = refs[0][group].astype(F32)
    for part in refs[1:-1]:
        total = total + part[group].astype(F32)
    refs[-1][...] = total.astype(BF16)


def add_group(offset, beam_pos, parts):
    return pl.pallas_call(
        functools.partial(add_kernel, offset),
        in_specs=[SCALAR] + [CHIP] * len(parts),
        out_specs=CHIP,
        out_shape=pltpu.VMEM((16, 16, 128), BF16),
        compiler_params=pltpu.CompilerParams(vmem_limit_bytes=SMALL_LIMIT),
        name="add_group",
    )(beam_pos, *[on_chip(part) for part in parts])


def merge_kernel(beam_pos, *refs):
    del beam_pos
    parts, out, stage = refs[:4], refs[4], refs[5]
    scale = 1.0 / math.sqrt(P_SIZE * Q * STATIONS)
    for n, part in enumerate(parts):

        @pl.when(pl.program_id(0) == n)
        def _(part=part):
            for i in range(16):
                stage[pl.ds(i, 16, stride=BEAM_ROWS), :] = part[i].astype(F32) * scale
            for beam in range(16):
                row = beam * BEAM_ROWS
                out[beam] = stage[row : row + 16, :]


def merge(beam_pos, parts):
    return pl.pallas_call(
        merge_kernel,
        grid_spec=pltpu.PrefetchScalarGridSpec(
            num_scalar_prefetch=1,
            grid=(4,),
            in_specs=[CHIP] * 4,
            out_specs=pl.BlockSpec((16, 16, 128), lambda n, pos: (0, pos[0] ^ n, 0)),
            scratch_shapes=[pltpu.VMEM((16 * BEAM_ROWS, 128), F32)],
        ),
        out_shape=jax.ShapeDtypeStruct((16, 64, 128), F32),
        compiler_params=pltpu.CompilerParams(vmem_limit_bytes=SMALL_LIMIT),
        name="merge",
    )(beam_pos, *[on_chip(part) for part in parts])


def keep_kernel(beam_pos, owners, models, out):
    out[...] = models[owners[beam_pos[0]]]


def keep_owner(beam_pos, owners, models):
    return pl.pallas_call(
        keep_kernel,
        in_specs=[SCALAR, SCALAR, CHIP],
        out_specs=CHIP,
        out_shape=pltpu.VMEM(models.shape[1:], F32),
        compiler_params=pltpu.CompilerParams(vmem_limit_bytes=SMALL_LIMIT),
        name="keep_owner",
    )(beam_pos, owners, on_chip(models))


def station_pick(station_map):
    starts = [(yh * 4 + zh) * 64 for zh in range(4) for yh in range(2)]
    phys = jnp.concatenate([station_map[n : n + 64] for n in starts])
    return (jnp.arange(STATIONS, dtype=jnp.int32)[:, None] == phys[None, :]).astype(F32)


def pick_columns(values, pick):
    return jnp.dot(values, pick, precision=lax.Precision.HIGHEST)


def shift(value, axis, offset):
    return lax.ppermute(value, axis, [(n, (n + offset) % 4) for n in range(4)])


def swap(value, axes, offset):
    return lax.ppermute(value, axes, [(n, n ^ offset) for n in range(4)])


def on_device(voltages, fir_taps, delays, taper, station_map, beam_order, owners):
    yh, zh, zl, x, yl, c = [lax.axis_index(name) for name in AXES]
    volts = voltages.reshape(2, 2, 75 * P_SIZE, Q).transpose(0, 2, 1, 3).reshape(2, 75, 128, Q)
    slots = delays.shape[1]
    beam_pos = yl * 2 + c

    pick = station_pick(station_map)
    model = pick_columns(delays[0], pick).reshape(slots, 4, 128).transpose(1, 0, 2)
    model = jnp.broadcast_to(model[None, :, None], (2, 4, 8, slots, 128))
    models = lax.all_to_all(model.reshape(64, slots, 128), AXES[:4], 0, 0, tiled=True)
    spectra = channelize(volts, fir_taps)
    models, spectra = lax.optimization_barrier((models, spectra))
    pos = beam_pos.astype(jnp.int32)[None]
    delay = keep_owner(pos, owners, models)
    delay, spectra = lax.optimization_barrier((delay, spectra))
    models = [delay] + [swap(delay, ("yl", "c"), n) for n in range(1, 4)]
    turned = lax.all_to_all(spectra.reshape(64, 4, 64, 128), TURN, 0, 0, tiled=True)

    for bit in (1, 2):
        odd = beam_pos & bit != 0
        models = [jnp.where(odd, models[n ^ bit], models[n]) for n in range(4)]
    delay = jnp.concatenate(models, axis=0)
    gain = pick_columns(taper[beam_order], pick)
    gain = lax.dynamic_slice_in_dim(gain, zh * 128, 128, 1)
    first_chan = yh * 2048 + zl * 256 + x * 64 + beam_pos * 16
    unit = TWO_PI / (P_SIZE * Q)
    step = jnp.stack((jnp.cos(delay * unit), jnp.sin(delay * unit)))

    def beams_for(offset):
        target = (zh + offset) % 4
        phase = delay * (first_chan + 512 * target).astype(F32) * unit
        base = jnp.stack((gain * jnp.cos(phase), gain * jnp.sin(phase)))
        return form_beams(target[None], turned, base, step)

    far_re, far_im = beams_for(2)
    far_re, far_im = shift(far_re, "zh", 1), shift(far_im, "zh", 3)
    up_re, up_im = beams_for(1)
    up_im = shift(up_im, "zh", 1)
    down_re, down_im = beams_for(3)
    down_re = shift(down_re, "zh", 3)
    own = beams_for(0)
    up_re = shift(add_pair(up_re, far_re), "zh", 1)
    down_im = shift(add_pair(down_im, far_im), "zh", 3)
    outs = []
    for parts in ((own[0], up_re, down_re), (own[1], up_im, down_im)):
        quarters = {}
        for n in (2, 3, 1, 0):
            quarter = add_group(n, pos, parts)
            quarters[n] = swap(quarter, ("yl", "c"), n) if n else quarter
        outs.append([quarters[n] for n in range(4)])
    return tuple(merge(pos, quarters) for quarters in outs)


def solution(mesh):
    torus = Mesh(mesh.devices.reshape(SIZES), AXES)
    stn, beam = AXES[:4], AXES[4:]
    return jax.shard_map(
        on_device,
        mesh=torus,
        in_specs=(P(AXES, None, None), P(), P(stn, beam, None), P(), P(), P(), P()),
        out_specs=(P(beam, stn, None), P(beam, stn, None)),
        check_vma=False,
    )
```
